32 devices in a mesh: dp: 8 (over z, x), expert: 4 (over y, core).
Axes of the slice: x: 2, y: 2, z: 4, core: 2. Of those that a mesh axis runs over, the one named last changes fastest.
Arguments:
- x_spans: bfloat16 [8, 8, 4, 16, 1536], P('dp', None, 'expert'), may hold values from -36 to 36
- crops: int32 [8, 4, 128, 1], P('dp', 'expert'), may hold values from 0 to 7; in each aligned block of 128 rows (0 to 127, 128 to 255, ..., all dimensions but the last counted through in order) at most 32 rows name the same one
- decay: float32 [8, 4, 128, 24], P('dp', 'expert'), may hold values from -1 to 0
- attn_gain: bfloat16 [1536], replicated, may hold values from 0.099609375 to 1.8984375
- w_query: bfloat16 [1536, 1536], replicated, may hold values from -0.15625 to 0.15625
- w_key: bfloat16 [1536, 1536], replicated, may hold values from -0.15625 to 0.15625
- w_value: bfloat16 [1536, 1536], replicated, may hold values from -0.15625 to 0.15625
- head_gain: bfloat16 [1536], replicated, may hold values from 0.099609375 to 1.8984375
- w_out: bfloat16 [1536, 1536], replicated, may hold values from -0.15625 to 0.15625
- moe_gain: bfloat16 [1536], replicated, may hold values from 0.099609375 to 1.8984375
- w_gate: bfloat16 [8, 1536, 6144], P('expert', None, 'dp'), may hold values from -0.15625 to 0.15625
- w_up: bfloat16 [8, 1536, 6144], P('expert', None, 'dp'), may hold values from -0.15625 to 0.15625
- w_down: bfloat16 [8, 6144, 1536], P('expert', 'dp'), may hold values from -0.078125 to 0.078125
Outputs:
- layer_out: bfloat16 [8, 4, 128, 1536], P('dp', 'expert')
The draws below stay inside these ranges and needn't reach their ends.
Inputs may be any that keep to these rules, and one draw needn't show every extreme that they name: `crops`: within the tokens of one plot no crop is named more than 32 times, and some plot names some crop exactly 32 times.
All inputs are finite; a program needn't handle non-finite values.
Results may differ from the reference program's by a relative error of at most 0.012.
Values may be sent and summed in bfloat16 or wider, within the bound.
A program may use at most 128 MiB of HBM per device.

```python
import math
import jax
import jax.numpy as jnp
import numpy as np
from jax import lax

D = 1536
HEADS = 24
HEAD_DIM = 64
FF = 6144
EXPERTS = 8
VISITS_EACH_TILE = 128
CAP = 32
SPANS = 8
PARCEL_DOWNWARD = 8
PARCEL_ACROSS = 4
PLOTS = 32
CLEN = 16
HID_DEV = 768
N_DP = 8


def draw_x_spans(key, part):
    noise_seed_splits = jax.random.split(key, 3)
    full_shape = (SPANS, PARCEL_DOWNWARD, PARCEL_ACROSS, CLEN, D)
    row_scale = jnp.exp(jax.random.uniform(noise_seed_splits[1], (SPANS, PARCEL_DOWNWARD, PARCEL_ACROSS, CLEN, 1), minval=math.log(0.3), maxval=math.log(3.0)))
    col_scale = jnp.exp(jax.random.uniform(noise_seed_splits[2], (D,), minval=math.log(0.3), maxval=math.log(3.0)))
    noise_base = jax.random.truncated_normal(noise_seed_splits[0], -4.0, 4.0, full_shape)
    return (noise_base * row_scale * col_scale).astype(jnp.bfloat16)


def draw_decay(key, part):
    noise_seed_splits = jax.random.split(key, 7)
    full_shape = (PARCEL_DOWNWARD, PARCEL_ACROSS, VISITS_EACH_TILE, HEADS)
    fast_share = 0.5
    fast_heads = jax.random.uniform(noise_seed_splits[0], (HEADS,)) < fast_share
    fast_rate = jax.random.uniform(noise_seed_splits[1], (HEADS,), minval=1.0 / 50.0, maxval=1.0 / 30.0)
    slow_rate = jax.random.uniform(noise_seed_splits[2], (HEADS,), minval=0.1, maxval=0.4) / VISITS_EACH_TILE
    channel_fading_speed = jnp.where(fast_heads, fast_rate, slow_rate)
    parcel_scaling = jnp.exp(jax.random.uniform(noise_seed_splits[3], (PARCEL_DOWNWARD, PARCEL_ACROSS, 1, HEADS), minval=math.log(0.5), maxval=math.log(2.0)))
    noise_jitter = jax.random.uniform(noise_seed_splits[4], full_shape, minval=0.5, maxval=1.5)
    spike_switched_on = jax.random.uniform(noise_seed_splits[5], (PARCEL_DOWNWARD, PARCEL_ACROSS, VISITS_EACH_TILE, 1)) < 2.0 / VISITS_EACH_TILE
    spike_duration = jax.random.uniform(noise_seed_splits[6], (PARCEL_DOWNWARD, PARCEL_ACROSS, VISITS_EACH_TILE, 1), minval=0.22, maxval=0.69)
    return (-(channel_fading_speed * parcel_scaling * noise_jitter) - jnp.where(spike_switched_on, spike_duration, 0.0)).astype(jnp.float32)


def block_levels(rng, shape, shards, least, largest):
    def one(dim, blocks):
        draws = jax.random.uniform(jax.random.fold_in(jax.random.fold_in(rng, 6), dim), (blocks,), jnp.float32, least / len(shards), largest / len(shards))
        return jnp.repeat(jnp.exp(draws), shape[dim] // blocks).reshape((-1,) + (1,) * (len(shape) - dim - 1))

    level = one(*shards[0])
    for cut in shards[1:]:
        level = level * one(*cut)
    return level


def routed_block(stream_key, own, number, rows, amount, top, reach, skew):
    sequence = jax.random.permutation(stream_key, amount)
    heavy_load, usual = load_shares(amount, rows * top, reach, skew, True), load_shares(amount, rows * top, reach, skew, False)
    places = jnp.arange(amount)

    def named(tallies, turn):
        used = int((tallies > 0).sum())
        fixed = max(1, used // 4)
        shifted = fixed + (places - fixed + turn * (used - fixed)) % max(1, amount - fixed)
        return jnp.zeros((amount,), jnp.int32).at[sequence[jnp.where(places < fixed, places, shifted)]].set(jnp.asarray(tallies, jnp.int32))

    tallies = jnp.where(number % 4 == 0, named(heavy_load, number // 4), named(usual, number - number // 4 - 1))
    mixed = jax.random.permutation(jax.random.fold_in(own, 3), amount)
    donor, receiver = mixed[0:amount // 2 * 2:2], mixed[1:amount // 2 * 2:2]
    margin = jnp.minimum(tallies[donor] - 1, reach - tallies[receiver]) // 2
    margin = jnp.where((donor == sequence[0]) | (receiver == sequence[0]) | (tallies[receiver] == 0), 0, jnp.maximum(margin, 0))
    shifted = jax.random.randint(jax.random.fold_in(own, 4), (amount // 2,), 0, 1 << 20) % (margin + 1)
    tallies = tallies.at[donor].add(-shifted).at[receiver].add(shifted)
    members = jnp.searchsorted(jnp.cumsum(tallies), jnp.arange(rows * top), side="right").astype(jnp.int32)
    table = members.reshape(top, rows).T
    table = table[jax.random.permutation(jax.random.fold_in(own, 1), rows)]
    turn = jax.random.randint(jax.random.fold_in(own, 2), (rows, 1), 0, top)
    return jnp.take_along_axis(table, (jnp.arange(top)[None, :] + turn) % top, axis=1)


def load_shares(count, total, bound, slope, full):
    portions = [(1 << 20) // math.isqrt(rank ** slope) + 1 for rank in range(1, count + 1)]
    largest = bound if full else min(bound, max(-(-total // count), total * portions[0] // sum(portions)))
    least = 1 if total - largest >= count - 1 else 0
    counts, rest = [largest] + [least] * (count - 1), total - largest - least * (count - 1)
    while rest > 0:
        free = [i for i in range(1, count) if counts[i] < largest] or [i for i in range(1, count) if counts[i] < bound]
        whole, left = sum([portions[i] for i in free]), rest
        for i in free:
            addition = min(bound - counts[i], max(1, left * portions[i] // whole), rest)
            counts[i] = counts[i] + addition
            rest = rest - addition
    return np.array(counts)


def normal_values(key, shape, spread, reach, cuts=(), kind=jnp.bfloat16):
    result = jax.random.normal(key, shape, jnp.float32) * spread
    if len(cuts) > 0:
        result = block_levels(key, shape, cuts, -0.22, 0.18) * result
    return jnp.clip(result, min=-reach, max=reach).astype(kind)


def setup_inputs(seed: int = 0) -> dict:
    arg_keys = jax.random.split(jax.random.key(seed), 14)
    x_spans = draw_x_spans(jax.random.fold_in(arg_keys[13], 71), 0)
    crops_keys = jax.random.split(jax.random.fold_in(arg_keys[1], 1), PARCEL_DOWNWARD * PARCEL_ACROSS * VISITS_EACH_TILE // VISITS_EACH_TILE)
    crops_turns = jax.random.permutation(jax.random.fold_in(arg_keys[1], 3), PARCEL_DOWNWARD * PARCEL_ACROSS * VISITS_EACH_TILE // VISITS_EACH_TILE)
    crops = jax.vmap(lambda own, number: routed_block(jax.random.fold_in(arg_keys[1], 2), own, number, VISITS_EACH_TILE, EXPERTS, 1, CAP, 2))(crops_keys, crops_turns).reshape((PARCEL_DOWNWARD, PARCEL_ACROSS, VISITS_EACH_TILE, 1))
    decay = draw_decay(jax.random.fold_in(arg_keys[13], 71), 0)
    attn_gain = jnp.clip(1.0 + 0.18 * jax.random.normal(arg_keys[3], (D,), jnp.float32), 0.099609375, 1.8984375).astype(jnp.bfloat16)
    w_query = normal_values(arg_keys[4], (D, D), D ** -0.5, 0.15625)
    w_key = normal_values(arg_keys[5], (D, D), D ** -0.5, 0.15625)
    w_value = normal_values(arg_keys[6], (D, D), D ** -0.5, 0.15625)
    head_gain = jnp.clip(1.0 + 0.18 * jax.random.normal(arg_keys[7], (D,), jnp.float32), 0.099609375, 1.8984375).astype(jnp.bfloat16)
    w_out = normal_values(arg_keys[8], (D, D), D ** -0.5, 0.15625)
    moe_gain = jnp.clip(1.0 + 0.18 * jax.random.normal(arg_keys[9], (D,), jnp.float32), 0.099609375, 1.8984375).astype(jnp.bfloat16)
    w_gate = normal_values(arg_keys[10], (EXPERTS, D, FF), D ** -0.5, 0.15625, ((0, 4), (2, 8)))
    w_up = normal_values(arg_keys[11], (EXPERTS, D, FF), D ** -0.5, 0.15625, ((0, 4), (2, 8)))
    w_down = normal_values(arg_keys[12], (EXPERTS, FF, D), FF ** -0.5, 0.078125, ((0, 4), (1, 8)))
    return dict(x_spans=x_spans, crops=crops, decay=decay, attn_gain=attn_gain, w_query=w_query, w_key=w_key, w_value=w_value, head_gain=head_gain, w_out=w_out, moe_gain=moe_gain, w_gate=w_gate, w_up=w_up, w_down=w_down)


def rms_scale(values, width_eps):
    return lax.rsqrt(lax.optimization_barrier(jnp.mean(values * values, axis=-1, keepdims=True)) + width_eps)

def reference(x_spans, crops, decay, attn_gain, w_query, w_key, w_value, head_gain, w_out, moe_gain, w_gate, w_up, w_down):
    sequences = jnp.transpose(x_spans, (1, 2, 0, 3, 4)).reshape(PLOTS, VISITS_EACH_TILE, D)
    forgets = decay.reshape(PLOTS, VISITS_EACH_TILE, HEADS)

    def attend(packed):
        tokens, forget = packed
        widened = tokens.astype(jnp.float32)
        normed = (widened * rms_scale(widened, 1e-05) * attn_gain.astype(jnp.float32)).astype(jnp.bfloat16)
        query = jnp.dot(normed, w_query, preferred_element_type=jnp.float32).astype(jnp.bfloat16)
        key_vecs = jnp.dot(normed, w_key, preferred_element_type=jnp.float32).astype(jnp.bfloat16)
        value_vecs = jnp.dot(normed, w_value, preferred_element_type=jnp.float32).astype(jnp.bfloat16)
        query_heads = query.astype(jnp.float32).reshape(VISITS_EACH_TILE, HEADS, HEAD_DIM)
        key_heads = key_vecs.astype(jnp.float32).reshape(VISITS_EACH_TILE, HEADS, HEAD_DIM)
        value_heads = value_vecs.astype(jnp.float32).reshape(VISITS_EACH_TILE, HEADS, HEAD_DIM)
        cumulative = jnp.cumsum(forget, axis=0)
        scores = jnp.einsum('thd,shd->hts', query_heads, key_heads, precision=lax.Precision.HIGHEST)
        by_head = cumulative.T
        spread_vals = by_head[:, :, None] - by_head[:, None, :]
        causal = jnp.arange(VISITS_EACH_TILE)[:, None] >= jnp.arange(VISITS_EACH_TILE)[None, :]
        weights = jnp.exp(jnp.where(causal[None], spread_vals, -jnp.inf))
        mixed = jnp.einsum('hts,shd->thd', scores * weights, value_heads, precision=lax.Precision.HIGHEST)
        head_scale = head_gain.astype(jnp.float32).reshape(HEADS, HEAD_DIM)
        head_normed = (mixed * rms_scale(mixed, 1e-05) * head_scale).reshape(VISITS_EACH_TILE, D).astype(jnp.bfloat16)
        resid = (widened + jnp.dot(head_normed, w_out, preferred_element_type=jnp.float32)).astype(jnp.bfloat16)
        resid_wide = resid.astype(jnp.float32)
        routed = (resid_wide * rms_scale(resid_wide, 1e-05) * moe_gain.astype(jnp.float32)).astype(jnp.bfloat16)
        return (resid, routed)
    resid, routed = lax.map(attend, (sequences, forgets))
    crop_ids = crops.reshape(PLOTS, VISITS_EACH_TILE).astype(jnp.int32)
    onehot = (crop_ids[:, :, None] == jnp.arange(EXPERTS, dtype=jnp.int32)[None, None, :]).astype(jnp.int32)
    slot_ids = lax.optimization_barrier(jnp.sum((jnp.cumsum(onehot, axis=1) - onehot) * onehot, axis=-1)).astype(jnp.int32)
    plot_ids = jnp.broadcast_to(jnp.arange(PLOTS, dtype=jnp.int32)[:, None], (PLOTS, VISITS_EACH_TILE))
    buffer = jnp.zeros((EXPERTS, PLOTS, CAP, D), jnp.bfloat16).at[crop_ids, plot_ids, slot_ids].set(routed)

    def expert(operands):
        row_block, gate_matrix, up_matrix, down_matrix = operands
        flattened = row_block.reshape(PLOTS * CAP, D)
        gate_act = jnp.dot(flattened, gate_matrix, preferred_element_type=jnp.float32)
        up_act = jnp.dot(flattened, up_matrix, preferred_element_type=jnp.float32)
        hidden = (jax.nn.silu(gate_act) * up_act).astype(jnp.bfloat16)
        accumulated = jnp.zeros((PLOTS * CAP, D), jnp.float32)
        for group_index in range(N_DP):
            lower = group_index * HID_DEV
            partial_value = jnp.dot(hidden[:, lower:lower + HID_DEV], down_matrix[lower:lower + HID_DEV], preferred_element_type=jnp.float32).astype(jnp.bfloat16)
            partial_value = lax.optimization_barrier(partial_value)
            accumulated = accumulated + partial_value.astype(jnp.float32)
        return accumulated.astype(jnp.bfloat16).reshape(PLOTS, CAP, D)
    outputs = lax.map(expert, (buffer, w_gate, w_up, w_down))
    returned = outputs[crop_ids, plot_ids, slot_ids]
    layer_sum = (resid.astype(jnp.float32) + returned.astype(jnp.float32)).astype(jnp.bfloat16)
    return layer_sum.reshape(PARCEL_DOWNWARD, PARCEL_ACROSS, VISITS_EACH_TILE, D)
```

```python
import jax
import jax.numpy as jnp
from jax import lax
from jax.experimental import pallas as pl
from jax.experimental.pallas import tpu as pltpu
from jax.sharding import PartitionSpec as P

D = 1536
HEADS = 24
HEAD_DIM = 64
EXPERTS = 8
LAYER = 4
NZ = 4
NX = 2
NY = 2
NC = 2
CHIPS = NZ * NX * NY
Z_UP, Z_DOWN, BY_X, BY_Y, CORE = range(5)


def place():
    dp, expert = lax.axis_index("dp"), lax.axis_index("expert")
    return dp // NX, dp % NX, expert // NC, expert % NC


def device(z, x, y, c):
    return (z * NX + x, y * NC + c)


def plot_of(z, x, y, c):
    return (z * NX + x) * (NY * NC) + y * NC + c


def chip_of(z, x, y):
    return (z * NX + x) * NY + y


def partner(kind, z, x, y, c):
    if kind == Z_UP:
        return device(z + 1, x, y, c)
    if kind == Z_DOWN:
        return device(z - 1, x, y, c)
    if kind == BY_X:
        return device(z, 1 - x, y, c)
    if kind == BY_Y:
        return device(z, x, 1 - y, c)
    return device(z, x, y, 1 - c)


def only_if(condition, body):
    if condition is None:
        body()
    else:
        pl.when(condition)(body)


def exists(kind, z):
    return {Z_UP: z < NZ - 1, Z_DOWN: z > 0}.get(kind)


def greet(z, x, y, c):
    barrier = pltpu.get_barrier_semaphore()
    for kind in range(5):

        def signal(kind=kind):
            pl.semaphore_signal(
                barrier,
                inc=1,
                device_id=partner(kind, z, x, y, c),
                device_id_type=pl.DeviceIdType.MESH,
            )

        only_if(exists(kind, z), signal)
    pl.semaphore_wait(barrier, 3 + jnp.where(z > 0, 1, 0) + jnp.where(z < NZ - 1, 1, 0))


def slot_positions(crop_ids, capacity):
    length = crop_ids.shape[0]
    same = crop_ids[:, None] == crop_ids[None, :]
    earlier = jnp.arange(length)[None, :] < jnp.arange(length)[:, None]
    slot_ids = jnp.sum(jnp.logical_and(same, earlier).astype(jnp.int32), axis=1)
    return crop_ids * capacity + slot_ids


def order_of(i, z):
    nearer = z + 1 - 2 * (z % 2)
    far = jnp.where(z < 2, 2, 1)
    last = jnp.where(z < 2, 3, 0)
    return jnp.where(i == 0, z, jnp.where(i == 1, nearer, jnp.where(i == 2, far, last)))


def experts_kernel(
    pos_in_ref,
    own_ref,
    w_gate_any,
    w_up_any,
    w_down_any,
    out_ref,
    tokens,
    pos,
    w_gate,
    w_up,
    w_down,
    packed,
    terms,
    core_buf,
    first_buf,
    second_buf,
    up_buf,
    down_buf,
    send_sem,
    core_send,
    arrive_sem,
    core_arrive,
    pos_send,
    pos_arrive,
    pos_z_send,
    pos_z_arrive,
    weight_sem,
    term_sem,
    first_sem,
    second_sem,
    chain_sem,
):
    z, x, y, c = place()
    length = own_ref.shape[0]
    half = length // 2
    experts, _, width = w_gate.shape
    capacity = length // 4
    held = experts * capacity
    base = (y * NC + c) * held
    mine = chip_of(z, x, y)

    loads = [
        pltpu.make_async_copy(src, dst, weight_sem.at[k])
        for k, (src, dst) in enumerate(
            ((w_gate_any, w_gate), (w_up_any, w_up), (w_down_any, w_down))
        )
    ]
    for load in loads:
        load.start()
    tokens[c, mine] = own_ref[...]
    pos[z, x, y, c] = pos_in_ref[...]
    greet(z, x, y, c)

    def remote(src, dst, send, arrive, kind):
        return pltpu.make_async_remote_copy(
            src_ref=src,
            dst_ref=dst,
            send_sem=send,
            recv_sem=arrive,
            device_id=partner(kind, z, x, y, c),
            device_id_type=pl.DeviceIdType.MESH,
        )

    def rows(h):
        return pl.ds(h * half, half)

    def copy(h, kind, bz, bx, by):
        chip = chip_of(bz, bx, by)
        block = tokens.at[c, chip, rows(h)]
        if kind == CORE:
            return remote(block, block, core_send.at[bz], core_arrive.at[bz], CORE)
        return remote(block, block, send_sem.at[kind], arrive_sem.at[h, chip], kind)

    def send(h, kind, bz, bx, by):
        only_if(exists(kind, z), lambda: copy(h, kind, bz, bx, by).start())

    def arrive(h, bz, bx, by):
        copy(h, BY_X, bz, bx, by).wait_recv()

    middle = (BY_X, BY_Y)
    last = (BY_Y, BY_X)

    def spots(distance, body):
        if isinstance(distance, int) and distance == 0:
            body(z, None)
            return
        for sign, way in ((-1, Z_UP), (1, Z_DOWN)):
            bz = z + sign * distance
            inside = jnp.logical_and(bz >= 0, bz < NZ)
            pl.when(inside)(lambda bz=bz, way=way: body(bz, way))

    def along_z(distance):
        def body(bz, way):
            for h in range(2):
                arrive(h, bz, x, y)
                for kind in (way, middle[h], last[h], CORE):
                    send(h, kind, bz, x, y)

        spots(distance, body)

    def middles(distance):
        def body(bz, _):
            for h in range(2):
                bx, by = (1 - x, y) if h == 0 else (x, 1 - y)
                arrive(h, bz, bx, by)
                for kind in (last[h], CORE):
                    send(h, kind, bz, bx, by)

        spots(distance, body)

    def lasts(distance):
        def body(bz, _):
            for h in range(2):
                bx, by = (x, 1 - y) if h == 0 else (1 - x, y)
                arrive(h, bz, bx, by)
                send(h, CORE, bz, bx, by)
            for h in range(2):
                arrive(h, bz, 1 - x, 1 - y)
                send(h, CORE, bz, 1 - x, 1 - y)

        spots(distance, body)

    def core_wait(bz):
        landed = tokens.at[1 - c, pl.ds(bz * LAYER, LAYER)]
        remote(landed, landed, core_send.at[bz], core_arrive.at[bz], CORE).wait_recv()

    def pos_copy(step):
        block = (pos.at[z, x, y, c], pos.at[z, x, y], pos.at[z, x])[step]
        kind = (CORE, BY_Y, BY_X)[step]
        return remote(block, block, pos_send.at[step], pos_arrive.at[step], kind)

    def pos_landed(step):
        block = (pos.at[z, x, y, 1 - c], pos.at[z, x, 1 - y], pos.at[z, 1 - x])[step]
        kind = (CORE, BY_Y, BY_X)[step]
        remote(block, block, pos_send.at[step], pos_arrive.at[step], kind).wait_recv()

    def pos_z(bz, way):
        return remote(
            pos.at[bz], pos.at[bz], pos_z_send.at[way, bz], pos_z_arrive.at[bz], way
        )

    def pos_along(distance):
        def body(bz, way):
            pos_z(bz, Z_UP).wait_recv()
            only_if(exists(way, z), lambda: pos_z(bz, way).start())

        spots(distance, body)

    slots = lax.broadcasted_iota(jnp.int32, (held, length), 0) + base

    def select(bz, bx, by, core):
        hit = slots == pos[bz, bx, by, core, 0:1, :]
        return jnp.where(hit, 1.0, 0.0).astype(jnp.bfloat16)

    spread_over = [(bx, by) for bx in range(NX) for by in range(NY)]

    def pack(bz, core):
        for k, (bx, by) in enumerate(spread_over):
            picked = jnp.dot(
                select(bz, bx, by, core),
                tokens[core, chip_of(bz, bx, by)],
                preferred_element_type=jnp.float32,
            ).astype(jnp.bfloat16)
            for j in range(experts):
                packed[j, core * LAYER + k] = picked[j * capacity : (j + 1) * capacity]

    def run_expert(j):
        given = packed[j].reshape(NC * LAYER * capacity, D)
        gate_act = jnp.dot(given, w_gate[j], preferred_element_type=jnp.float32)
        up_act = jnp.dot(given, w_up[j], preferred_element_type=jnp.float32)
        hidden = (gate_act / (1.0 + jnp.exp(-gate_act)) * up_act).astype(jnp.bfloat16)
        packed[j] = (
            jnp.dot(hidden, w_down[j], preferred_element_type=jnp.float32)
            .astype(jnp.bfloat16)
            .reshape(NC * LAYER, capacity, D)
        )

    def unpack(bz, core):
        for k, (bx, by) in enumerate(spread_over):
            term = jnp.concatenate(
                [packed[j, core * LAYER + k] for j in range(experts)], axis=0
            )
            terms[core, chip_of(bz, bx, by)] = lax.dot_general(
                select(bz, bx, by, core),
                term,
                (((0,), (0,)), ((), ())),
                preferred_element_type=jnp.float32,
            ).astype(jnp.bfloat16)

    def term_copy(bz):
        layer = pl.ds(bz * LAYER, LAYER)
        return remote(
            terms.at[1 - c, layer],
            core_buf.at[layer],
            term_sem.at[0, bz],
            term_sem.at[1, bz],
            CORE,
        )

    first_kind, second_kind = (BY_Y, BY_X), (BY_X, BY_Y)

    def spot(h, first_other, second_other):
        first, second = (y, x) if h == 0 else (x, y)
        first = 1 - first if first_other else first
        second = 1 - second if second_other else second
        return (second, first) if h == 0 else (first, second)

    def first_copy(h, bz, second, src):
        target = first_buf.at[h, bz, second]
        return remote(
            src,
            target,
            first_sem.at[0, h, bz, second],
            first_sem.at[1, h, bz, second],
            first_kind[h],
        )

    def second_copy(h, bz, src):
        return remote(
            src, second_buf.at[h, bz], second_sem.at[0, h, bz], second_sem.at[1, h, bz], second_kind[h]
        )

    def chain_copy(h, bz, kind):
        block = (up_buf if kind == Z_UP else down_buf).at[h, bz]
        return remote(block, block, chain_sem.at[0, kind, h, bz], chain_sem.at[1, kind, h, bz], kind)

    def wide(ref, *index):
        return ref[index].astype(jnp.float32)

    def pair(bz):
        term_copy(bz).wait_recv()
        for first_other, second_other in ((1, 1), (1, 0), (0, 1), (0, 0)):
            for h in range(2):
                bx, by = spot(h, first_other, second_other)
                chip = chip_of(bz, bx, by)
                total = wide(core_buf, chip, rows(h)) + wide(terms, c, chip, rows(h))
                core_buf[chip, rows(h)] = total.astype(jnp.bfloat16)
                if first_other:
                    first_copy(
                        h, bz, bx if h == 0 else by, core_buf.at[chip, rows(h)]
                    ).start()

    def across(bz):
        for h in range(2):
            bx, by = spot(h, 0, 1)
            second = bx if h == 0 else by
            landed = first_buf.at[h, bz, second]
            first_copy(h, bz, second, landed).wait_recv()
            total = wide(first_buf, h, bz, second) + wide(core_buf, chip_of(bz, bx, by), rows(h))
            first_buf[h, bz, second] = total.astype(jnp.bfloat16)
            second_copy(h, bz, landed).start()

    def in_plane(h, bz):
        bx, by = spot(h, 0, 0)
        second = bx if h == 0 else by
        first_copy(h, bz, second, first_buf.at[h, bz, second]).wait_recv()
        second_copy(h, bz, second_buf.at[h, bz]).wait_recv()
        return (
            wide(first_buf, h, bz, second)
            + wide(core_buf, chip_of(bz, bx, by), rows(h))
            + wide(second_buf, h, bz)
        )

    def along(bz):
        for h in range(2):
            total = in_plane(h, bz)
            for buf, kind, goes, comes in (
                (up_buf, Z_UP, bz > z, z > 0),
                (down_buf, Z_DOWN, bz < z, z < NZ - 1),
            ):

                @pl.when(goes)
                def _(buf=buf, kind=kind, comes=comes):
                    @pl.when(comes)
                    def _():
                        chain_copy(h, bz, kind).wait_recv()
                        buf[h, bz] = (total + wide(buf, h, bz)).astype(jnp.bfloat16)

                    @pl.when(jnp.logical_not(comes))
                    def _():
                        buf[h, bz] = total.astype(jnp.bfloat16)

                    chain_copy(h, bz, kind).start()

    for h in range(2):
        for kind in (Z_UP, Z_DOWN, middle[h], last[h], CORE):
            send(h, kind, z, x, y)
    pos_copy(0).start()
    pos_landed(0)
    pos_copy(1).start()
    along_z(1)
    middles(0)
    pos_landed(1)
    pos_copy(2).start()
    along_z(2)
    middles(1)
    lasts(0)
    pos_landed(2)
    for way in (Z_UP, Z_DOWN):
        only_if(exists(way, z), lambda way=way: pos_z(z, way).start())
    core_wait(z)
    for load in loads:
        load.wait()

    def step(i, carry):
        bz = order_of(i, z)
        before = order_of(i - 1, z)
        pack(bz, 0)

        @pl.when(i < 1)
        def _():
            along_z(3)

        pack(bz, 1)

        @pl.when(i < 3)
        def _():
            middles(i + 2)

        run_expert(0)

        @pl.when(i > 0)
        def _():
            pair(before)

        run_expert(1)

        @pl.when(i < 3)
        def _():
            lasts(i + 1)

        unpack(bz, 1 - c)
        term_copy(bz).start()

        @pl.when(i > 0)
        def _():
            across(before)

        unpack(bz, c)

        @pl.when(i < 3)
        def _():
            pos_along(i + 1)
            core_wait(order_of(i + 1, z))

        return carry

    lax.fori_loop(0, NZ, step, 0)
    final = order_of(3, z)
    pair(final)
    low = z < 2
    edge = jnp.logical_or(z == 0, z == NZ - 1)
    along(jnp.where(edge, jnp.where(low, 1, 2), jnp.where(low, 2, 1)))
    across(final)
    along(jnp.where(edge, jnp.where(low, 2, 1), final))
    along(jnp.where(edge, final, jnp.where(low, 0, 3)))
    for h in range(2):
        total = in_plane(h, z)

        @pl.when(z == 0)
        def _():
            chain_copy(h, z, Z_DOWN).wait_recv()
            out_ref[rows(h)] = (total + wide(down_buf, h, z)).astype(jnp.bfloat16)

        @pl.when(z == NZ - 1)
        def _():
            chain_copy(h, z, Z_UP).wait_recv()
            out_ref[rows(h)] = (total + wide(up_buf, h, z)).astype(jnp.bfloat16)

        @pl.when(jnp.logical_and(z > 0, z < NZ - 1))
        def _():
            chain_copy(h, z, Z_DOWN).wait_recv()
            chain_copy(h, z, Z_UP).wait_recv()
            both = wide(up_buf, h, z) + wide(down_buf, h, z)
            out_ref[rows(h)] = (total + both).astype(jnp.bfloat16)

    def left(block, sem):
        remote(block, block, sem, sem, BY_X).wait_send()

    for kind in (BY_X, BY_Y):
        left(tokens.at[0, pl.ds(0, 3 * NZ // 2)], send_sem.at[kind])
    for count in range(1, NZ):
        pl.when(z == count - 1)(
            lambda count=count: left(tokens.at[0, pl.ds(0, count)], send_sem.at[Z_UP])
        )
        pl.when(z == NZ - count)(
            lambda count=count: left(tokens.at[0, pl.ds(0, count)], send_sem.at[Z_DOWN])
        )
    for step_ in range(3):
        pos_copy(step_).wait_send()
    for bz in range(NZ):
        layer = pl.ds(bz * LAYER, LAYER)
        left(tokens.at[0, layer], core_send.at[bz])
        left(terms.at[0, layer], term_sem.at[0, bz])
        for way, goes in ((Z_UP, bz <= z), (Z_DOWN, bz >= z)):
            only_if(
                jnp.logical_and(goes, exists(way, z)),
                lambda bz=bz, way=way: pos_z(bz, way).wait_send(),
            )
        for h in range(2):
            for second in range(2):
                left(first_buf.at[h, bz, second], first_sem.at[0, h, bz, second])
            left(second_buf.at[h, bz], second_sem.at[0, h, bz])
            for kind, goes in ((Z_UP, bz > z), (Z_DOWN, bz < z)):
                pl.when(goes)(
                    lambda h=h, bz=bz, kind=kind: left(
                        up_buf.at[h, bz], chain_sem.at[0, kind, h, bz]
                    )
                )


def routed_experts(routed, position, w_gate, w_up, w_down):
    length = routed.shape[0]
    capacity = length // 4
    half = length // 2
    local_count, _, width = w_gate.shape

    def vmem(*shape):
        return pltpu.VMEM(shape, jnp.bfloat16)

    dma = pltpu.SemaphoreType.DMA
    any_space = pl.BlockSpec(memory_space=pl.ANY)
    in_vmem = pl.BlockSpec(memory_space=pltpu.VMEM)
    return pl.pallas_call(
        experts_kernel,
        out_shape=jax.ShapeDtypeStruct((length, D), jnp.bfloat16),
        in_specs=[in_vmem, in_vmem, any_space, any_space, any_space],
        out_specs=in_vmem,
        scratch_shapes=[
            vmem(NC, CHIPS, length, D),
            pltpu.VMEM((NZ, NX, NY, NC, 8, length), jnp.int32),
            vmem(local_count, D, width),
            vmem(local_count, D, width),
            vmem(local_count, width, D),
            vmem(local_count, NC * LAYER, capacity, D),
            vmem(NC, CHIPS, length, D),
            vmem(CHIPS, length, D),
            vmem(2, NZ, 2, half, D),
            vmem(2, NZ, half, D),
            vmem(2, NZ, half, D),
            vmem(2, NZ, half, D),
            dma((4,)),
            dma((NZ,)),
            dma((2, CHIPS)),
            dma((NZ,)),
            dma((3,)),
            dma((3,)),
            dma((2, NZ)),
            dma((NZ,)),
            dma((3,)),
            dma((2, NZ)),
            dma((2, 2, NZ, 2)),
            dma((2, 2, NZ)),
            dma((2, 2, 2, NZ)),
        ],
        compiler_params=pltpu.CompilerParams(
            collective_id=0, has_side_effects=True, vmem_limit_bytes=60 * 1024 * 1024
        ),
    )(jnp.broadcast_to(position[None, :], (8, length)), routed, w_gate, w_up, w_down)


def rms_scale(values, width_eps):
    return lax.rsqrt(jnp.mean(values * values, axis=-1, keepdims=True) + width_eps)


def spread(buffers):
    return lax.all_gather(buffers, "dp", axis=0, tiled=True)


def deliver(buffers):
    return lax.all_to_all(buffers, "expert", split_axis=1, concat_axis=1, tiled=True)


def attend_kernel(
    tokens_ref,
    column_ref,
    line_ref,
    attn_gain_ref,
    query_ref,
    key_ref,
    value_ref,
    head_gain_ref,
    w_out_ref,
    moe_gain_ref,
    resid_ref,
    routed_ref,
    normed_ref,
    total_ref,
):
    step = pl.program_id(0)
    length = tokens_ref.shape[0]

    @pl.when(step == 0)
    def _():
        widened = tokens_ref[...].astype(jnp.float32)
        scaled = widened * rms_scale(widened, 1e-05) * attn_gain_ref[...].astype(jnp.float32)
        normed_ref[...] = scaled.astype(jnp.bfloat16)
        total_ref[...] = widened

    def project(ref):
        return jnp.dot(
            normed_ref[...], ref[...], preferred_element_type=jnp.float32
        ).astype(jnp.bfloat16)

    query, key_vecs, value_vecs = project(query_ref), project(key_ref), project(value_ref)
    lanes = 2 * HEAD_DIM
    first = lax.broadcasted_iota(jnp.int32, (length, lanes), 1) < HEAD_DIM
    later = lax.broadcasted_iota(jnp.int32, (length, length), 0)
    causal = later >= lax.broadcasted_iota(jnp.int32, (length, length), 1)
    outcome = []
    for pair in range(query.shape[1] // lanes):
        cut = slice(pair * lanes, (pair + 1) * lanes)
        mixed = []
        for side in range(2):
            head = 2 * pair + side
            mask = first if side == 0 else jnp.logical_not(first)
            chosen = jnp.where(mask, query[:, cut], jnp.zeros((), jnp.bfloat16))
            scores = lax.dot_general(
                chosen,
                key_vecs[:, cut],
                (((1,), (1,)), ((), ())),
                preferred_element_type=jnp.float32,
            )
            gap = column_ref[0, :, head : head + 1] - line_ref[0, head : head + 1, :]
            weighted = scores * jnp.exp(jnp.where(causal, gap, -jnp.inf))
            coarse = weighted.astype(jnp.bfloat16)
            fine = (weighted - coarse.astype(jnp.float32)).astype(jnp.bfloat16)
            mixed.append(
                jnp.dot(coarse, value_vecs[:, cut], preferred_element_type=jnp.float32)
                + jnp.dot(fine, value_vecs[:, cut], preferred_element_type=jnp.float32)
            )
        both = jnp.where(first, mixed[0], mixed[1])
        square = both * both
        scale = [
            lax.rsqrt(
                jnp.sum(jnp.where(mask, square, 0.0), axis=-1, keepdims=True) / HEAD_DIM + 1e-05
            )
            for mask in (first, jnp.logical_not(first))
        ]
        gain = head_gain_ref[:, cut].astype(jnp.float32)
        outcome.append((both * jnp.where(first, scale[0], scale[1]) * gain).astype(jnp.bfloat16))
    total_ref[...] += jnp.dot(
        jnp.concatenate(outcome, axis=1), w_out_ref[...], preferred_element_type=jnp.float32
    )

    @pl.when(step == pl.num_programs(0) - 1)
    def _():
        resid = total_ref[...].astype(jnp.bfloat16)
        resid_ref[...] = resid
        wide = resid.astype(jnp.float32)
        scaled = wide * rms_scale(wide, 1e-05) * moe_gain_ref[...].astype(jnp.float32)
        routed_ref[...] = scaled.astype(jnp.bfloat16)


def attend(
    tokens, forget, attn_gain, w_query, w_key, w_value, head_gain, w_out, moe_gain
):
    length = tokens.shape[0]
    steps = 6
    width = D // steps
    until = jnp.arange(length)[None, :] <= jnp.arange(length)[:, None]
    cumulative = jnp.dot(until.astype(jnp.float32), forget, precision=lax.Precision.HIGHEST)
    line = cumulative.T.reshape(steps, HEADS // steps, length)
    column = jnp.transpose(line, (0, 2, 1))

    def whole(*shape):
        return pl.BlockSpec(shape, lambda j: (0,) * len(shape))

    columns = pl.BlockSpec((D, width), lambda j: (0, j))
    return pl.pallas_call(
        attend_kernel,
        grid=(steps,),
        out_shape=(
            jax.ShapeDtypeStruct((length, D), jnp.bfloat16),
            jax.ShapeDtypeStruct((length, D), jnp.bfloat16),
        ),
        in_specs=[
            whole(length, D),
            pl.BlockSpec((1, length, HEADS // steps), lambda j: (j, 0, 0)),
            pl.BlockSpec((1, HEADS // steps, length), lambda j: (j, 0, 0)),
            whole(1, D),
            columns,
            columns,
            columns,
            pl.BlockSpec((1, width), lambda j: (0, j)),
            pl.BlockSpec((width, D), lambda j: (j, 0)),
            whole(1, D),
        ],
        out_specs=(whole(length, D), whole(length, D)),
        scratch_shapes=[
            pltpu.VMEM((length, D), jnp.bfloat16),
            pltpu.VMEM((length, D), jnp.float32),
        ],
        compiler_params=pltpu.CompilerParams(vmem_limit_bytes=56 * 1024 * 1024),
    )(
        tokens,
        column,
        line,
        attn_gain.reshape(1, D),
        w_query,
        w_key,
        w_value,
        head_gain.reshape(1, D),
        w_out,
        moe_gain.reshape(1, D),
    )


def on_device(
    x_spans,
    crops,
    decay,
    attn_gain,
    w_query,
    w_key,
    w_value,
    head_gain,
    w_out,
    moe_gain,
    w_gate,
    w_up,
    w_down,
):
    arrived = lax.all_to_all(x_spans, "dp", split_axis=1, concat_axis=0, tiled=True)
    length = arrived.shape[0] * arrived.shape[3]
    tokens = arrived.reshape(length, D)
    forget = decay.reshape(length, HEADS)
    crop_ids = crops.reshape(length)
    capacity = length // 4
    position = slot_positions(crop_ids, capacity)
    resid, routed = attend(
        tokens, forget, attn_gain, w_query, w_key, w_value, head_gain, w_out, moe_gain
    )
    resid_wide = resid.astype(jnp.float32)
    if lax.axis_size("dp") == NZ * NX and lax.axis_size("expert") == NY * NC:
        expert_out = routed_experts(routed, position, w_gate, w_up, w_down)
        layer_sum = (resid_wide + expert_out.astype(jnp.float32)).astype(jnp.bfloat16)
        return layer_sum.reshape(1, 1, length, D)
    select = (jnp.arange(EXPERTS * capacity, dtype=jnp.int32)[:, None] == position[None, :]).astype(
        jnp.bfloat16
    )
    packed = jnp.dot(select, routed, preferred_element_type=jnp.float32).astype(jnp.bfloat16)
    owners = lax.axis_size("expert")
    local_count = w_gate.shape[0]
    outgoing = packed.reshape(1, owners, EXPERTS * capacity // owners, D)
    gathered = spread(deliver(outgoing))
    sources = gathered.shape[0]
    grouped = gathered.reshape(sources, owners, local_count, capacity, D)
    gate_act = jnp.einsum("sojcd,jdf->sojcf", grouped, w_gate, preferred_element_type=jnp.float32)
    up_act = jnp.einsum("sojcd,jdf->sojcf", grouped, w_up, preferred_element_type=jnp.float32)
    hidden = (jax.nn.silu(gate_act) * up_act).astype(jnp.bfloat16)
    term = jnp.einsum("sojcf,jfd->sojcd", hidden, w_down, preferred_element_type=jnp.float32)
    summed = lax.psum_scatter(
        term.reshape(1 * lax.axis_size("dp"), owners, local_count * capacity, D).astype(
            jnp.bfloat16
        ),
        "dp",
        scatter_dimension=0,
        tiled=True,
    )
    own_sums = summed[0]
    returned = lax.all_to_all(own_sums, "expert", split_axis=0, concat_axis=0, tiled=True)
    flat_back = returned.reshape(EXPERTS * capacity, D)
    expert_out = jnp.einsum("pl,pd->ld", select, flat_back, preferred_element_type=jnp.float32)
    layer_sum = (resid_wide + expert_out).astype(jnp.bfloat16)
    return layer_sum.reshape(1, 1, length, D)


def solution(mesh):
    return jax.shard_map(
        on_device,
        mesh=mesh,
        in_specs=(
            P("dp", None, "expert", None, None),
            P("dp", "expert", None, None),
            P("dp", "expert", None, None),
            P(),
            P(),
            P(),
            P(),
            P(),
            P(),
            P(),
            P("expert", None, "dp"),
            P("expert", None, "dp"),
            P("expert", "dp", None),
        ),
        out_specs=P("dp", "expert", None, None),
        check_vma=False,
    )
```

```python
import functools

import jax
import jax.numpy as jnp
from jax import lax
from jax.experimental import pallas as pl
from jax.experimental.pallas import tpu as pltpu
from jax.sharding import PartitionSpec as P

D = 1536
HEADS = 24
HEAD_DIM = 64
EXPERTS = 8
LAYER = 4
NZ = 4
NX = 2
NY = 2
NC = 2
CHIPS = NZ * NX * NY
Z_UP, Z_DOWN, BY_X, BY_Y, CORE = range(5)


def place():
    dp, expert = lax.axis_index("dp"), lax.axis_index("expert")
    return dp // NX, dp % NX, expert // NC, expert % NC


def device(z, x, y, c):
    return (z * NX + x, y * NC + c)


def plot_of(z, x, y, c):
    return (z * NX + x) * (NY * NC) + y * NC + c


def chip_of(z, x, y):
    return (z * NX + x) * NY + y


def partner(kind, z, x, y, c):
    if kind == Z_UP:
        return device(z + 1, x, y, c)
    if kind == Z_DOWN:
        return device(z - 1, x, y, c)
    if kind == BY_X:
        return device(z, 1 - x, y, c)
    if kind == BY_Y:
        return device(z, x, 1 - y, c)
    return device(z, x, y, 1 - c)


def only_if(condition, body):
    if condition is None:
        body()
    else:
        pl.when(condition)(body)


def exists(kind, z):
    return {Z_UP: z < NZ - 1, Z_DOWN: z > 0}.get(kind)


def greet(z, x, y, c):
    barrier = pltpu.get_barrier_semaphore()
    for kind in range(5):

        def signal(kind=kind):
            pl.semaphore_signal(
                barrier,
                inc=1,
                device_id=partner(kind, z, x, y, c),
                device_id_type=pl.DeviceIdType.MESH,
            )

        only_if(exists(kind, z), signal)
    pl.semaphore_wait(barrier, 3 + jnp.where(z > 0, 1, 0) + jnp.where(z < NZ - 1, 1, 0))


def slot_positions(crop_ids, capacity):
    length = crop_ids.shape[0]
    same = crop_ids[:, None] == crop_ids[None, :]
    earlier = jnp.arange(length)[None, :] < jnp.arange(length)[:, None]
    slot_ids = jnp.sum(jnp.logical_and(same, earlier).astype(jnp.int32), axis=1)
    return crop_ids * capacity + slot_ids


def rms_scale(values, width_eps):
    return lax.rsqrt(jnp.mean(values * values, axis=-1, keepdims=True) + width_eps)


def spread(buffers):
    return lax.all_gather(buffers, "dp", axis=0, tiled=True)


def deliver(buffers):
    return lax.all_to_all(buffers, "expert", split_axis=1, concat_axis=1, tiled=True)


def attend_kernel(
    tokens_ref,
    column_ref,
    line_ref,
    attn_gain_ref,
    query_ref,
    key_ref,
    value_ref,
    head_gain_ref,
    w_out_ref,
    moe_gain_ref,
    resid_ref,
    routed_ref,
    normed_ref,
    total_ref,
):
    step = pl.program_id(0)
    length = tokens_ref.shape[0]

    @pl.when(step == 0)
    def _():
        widened = tokens_ref[...].astype(jnp.float32)
        scaled = widened * rms_scale(widened, 1e-05) * attn_gain_ref[...].astype(jnp.float32)
        normed_ref[...] = scaled.astype(jnp.bfloat16)
        total_ref[...] = widened

    def project(ref):
        return jnp.dot(
            normed_ref[...], ref[...], preferred_element_type=jnp.float32
        ).astype(jnp.bfloat16)

    query, key_vecs, value_vecs = project(query_ref), project(key_ref), project(value_ref)
    lanes = 2 * HEAD_DIM
    first = lax.broadcasted_iota(jnp.int32, (length, lanes), 1) < HEAD_DIM
    later = lax.broadcasted_iota(jnp.int32, (length, length), 0)
    causal = later >= lax.broadcasted_iota(jnp.int32, (length, length), 1)
    outcome = []
    for pair in range(query.shape[1] // lanes):
        cut = slice(pair * lanes, (pair + 1) * lanes)
        mixed = []
        for side in range(2):
            head = 2 * pair + side
            mask = first if side == 0 else jnp.logical_not(first)
            chosen = jnp.where(mask, query[:, cut], jnp.zeros((), jnp.bfloat16))
            scores = lax.dot_general(
                chosen,
                key_vecs[:, cut],
                (((1,), (1,)), ((), ())),
                preferred_element_type=jnp.float32,
            )
            gap = column_ref[0, :, head : head + 1] - line_ref[0, head : head + 1, :]
            weighted = scores * jnp.exp(jnp.where(causal, gap, -jnp.inf))
            coarse = weighted.astype(jnp.bfloat16)
            fine = (weighted - coarse.astype(jnp.float32)).astype(jnp.bfloat16)
            mixed.append(
                jnp.dot(coarse, value_vecs[:, cut], preferred_element_type=jnp.float32)
                + jnp.dot(fine, value_vecs[:, cut], preferred_element_type=jnp.float32)
            )
        both = jnp.where(first, mixed[0], mixed[1])
        square = both * both
        scale = [
            lax.rsqrt(
                jnp.sum(jnp.where(mask, square, 0.0), axis=-1, keepdims=True) / HEAD_DIM + 1e-05
            )
            for mask in (first, jnp.logical_not(first))
        ]
        gain = head_gain_ref[:, cut].astype(jnp.float32)
        outcome.append((both * jnp.where(first, scale[0], scale[1]) * gain).astype(jnp.bfloat16))
    total_ref[...] += jnp.dot(
        jnp.concatenate(outcome, axis=1), w_out_ref[...], preferred_element_type=jnp.float32
    )

    @pl.when(step == pl.num_programs(0) - 1)
    def _():
        resid = total_ref[...].astype(jnp.bfloat16)
        resid_ref[...] = resid
        wide = resid.astype(jnp.float32)
        scaled = wide * rms_scale(wide, 1e-05) * moe_gain_ref[...].astype(jnp.float32)
        routed_ref[...] = scaled.astype(jnp.bfloat16)


def attend(
    tokens, forget, attn_gain, w_query, w_key, w_value, head_gain, w_out, moe_gain
):
    length = tokens.shape[0]
    steps = 6
    width = D // steps
    until = jnp.arange(length)[None, :] <= jnp.arange(length)[:, None]
    cumulative = jnp.dot(until.astype(jnp.float32), forget, precision=lax.Precision.HIGHEST)
    line = cumulative.T.reshape(steps, HEADS // steps, length)
    column = jnp.transpose(line, (0, 2, 1))

    def whole(*shape):
        return pl.BlockSpec(shape, lambda j: (0,) * len(shape))

    columns = pl.BlockSpec((D, width), lambda j: (0, j))
    return pl.pallas_call(
        attend_kernel,
        grid=(steps,),
        out_shape=(
            jax.ShapeDtypeStruct((length, D), jnp.bfloat16),
            jax.ShapeDtypeStruct((length, D), jnp.bfloat16),
        ),
        in_specs=[
            whole(length, D),
            pl.BlockSpec((1, length, HEADS // steps), lambda j: (j, 0, 0)),
            pl.BlockSpec((1, HEADS // steps, length), lambda j: (j, 0, 0)),
            whole(1, D),
            columns,
            columns,
            columns,
            pl.BlockSpec((1, width), lambda j: (0, j)),
            pl.BlockSpec((width, D), lambda j: (j, 0)),
            whole(1, D),
        ],
        out_specs=(whole(length, D), whole(length, D)),
        scratch_shapes=[
            pltpu.VMEM((length, D), jnp.bfloat16),
            pltpu.VMEM((length, D), jnp.float32),
        ],
        compiler_params=pltpu.CompilerParams(vmem_limit_bytes=56 * 1024 * 1024),
    )(
        tokens,
        column,
        line,
        attn_gain.reshape(1, D),
        w_query,
        w_key,
        w_value,
        head_gain.reshape(1, D),
        w_out,
        moe_gain.reshape(1, D),
    )


def position_rows(crop, y, per_half, capacity):
    length = crop.shape[1]
    half = length // 2
    expert = lax.broadcasted_iota(jnp.int32, (EXPERTS, length), 0)
    hot = jnp.where(expert == crop, 1.0, 0.0)
    sooner = lax.broadcasted_iota(jnp.int32, (length, length), 0) < lax.broadcasted_iota(
        jnp.int32, (length, length), 1
    )
    ahead = jnp.dot(
        hot.astype(jnp.bfloat16),
        jnp.where(sooner, 1.0, 0.0).astype(jnp.bfloat16),
        preferred_element_type=jnp.float32,
    )
    slot = jnp.sum(hot * ahead, axis=0, keepdims=True)
    place_of = crop.astype(jnp.float32) * capacity + slot
    low_ahead = jnp.sum(jnp.where(expert < per_half, ahead, 0.0), axis=0, keepdims=True)
    low = crop < per_half
    low_count = jnp.sum(jnp.where(low, 1.0, 0.0), axis=1, keepdims=True)
    date = lax.broadcasted_iota(jnp.int32, (1, length), 1).astype(jnp.float32)
    rank = jnp.where(low, low_ahead, date - low_ahead)
    within = jnp.where(rank < half, half - 1 - rank, rank)
    crossed = jnp.where(within < half, within + half, within - half)
    row_for = (jnp.where(low, within, crossed), jnp.where(low, crossed, within))
    rows = lax.broadcasted_iota(jnp.int32, (length, length), 0).astype(jnp.float32)
    wide_place = jnp.broadcast_to(place_of, (EXPERTS, length)).astype(jnp.bfloat16)
    ordered = [
        lax.dot_general(
            wide_place,
            jnp.where(rows == row, 1.0, 0.0).astype(jnp.bfloat16),
            (((1,), (1,)), ((), ())),
            preferred_element_type=jnp.float32,
        )[:1]
        for row in row_for
    ]
    own_row = jnp.where(y == 0, row_for[0], row_for[1])
    count = jnp.broadcast_to(low_count, (1, length))
    lines = (ordered[0], ordered[1], own_row, count)
    place_in = jnp.where(rows == own_row, 1.0, 0.0).astype(jnp.bfloat16)
    return lines, place_in


def attend_heads(query, key_vecs, value_vecs, column, line, gain):
    length = query.shape[0]
    lanes = 2 * HEAD_DIM
    first = lax.broadcasted_iota(jnp.int32, (length, lanes), 1) < HEAD_DIM
    later = lax.broadcasted_iota(jnp.int32, (length, length), 0)
    causal = later >= lax.broadcasted_iota(jnp.int32, (length, length), 1)
    none = jnp.zeros((), jnp.bfloat16)
    outcome = []
    for pair in range(query.shape[1] // lanes):
        cut = slice(pair * lanes, (pair + 1) * lanes)
        chosen = query[:, cut]
        both_heads = jnp.concatenate(
            [jnp.where(first, chosen, none), jnp.where(first, none, chosen)], axis=0
        )
        scores = lax.dot_general(
            both_heads, key_vecs[:, cut], (((1,), (1,)), ((), ())), preferred_element_type=jnp.float32
        )
        weighted = []
        for side in range(2):
            head = 2 * pair + side
            gap = column[:, head : head + 1] - line[head : head + 1, :]
            fade = jnp.exp(jnp.where(causal, gap, -jnp.inf))
            weighted.append(
                (scores[side * length : (side + 1) * length] * fade).astype(jnp.bfloat16)
            )
        mixed = jnp.dot(
            jnp.concatenate(weighted, axis=0), value_vecs[:, cut], preferred_element_type=jnp.float32
        )
        both = jnp.where(first, mixed[:length], mixed[length:])
        square = both * both
        scale = [
            lax.rsqrt(jnp.sum(part, axis=-1, keepdims=True) / HEAD_DIM + 1e-05)
            for part in (jnp.where(first, square, 0.0), jnp.where(first, 0.0, square))
        ]
        outcome.append((both * jnp.where(first, scale[0], scale[1]) * gain[:, cut]).astype(jnp.bfloat16))
    return jnp.concatenate(outcome, axis=1)


def attend_here_kernel(
    x_any,
    crop_ref,
    decay_ref,
    attn_gain_ref,
    head_gain_ref,
    moe_gain_ref,
    query_any,
    key_any,
    value_any,
    w_out_any,
    resid_ref,
    routed_ref,
    info_ref,
    need_ref,
    tokens,
    normed,
    total_ref,
    padded,
    head_gain_rows,
    line_ref,
    column_ref,
    w_query,
    w_key,
    w_value,
    w_out,
    weight_sem,
    stay_sem,
    x_sem,
    info_sem,
    pass_sem,
):
    z, x, y, c = place()
    spot, column_of = z * NX + x, y * NC + c
    spots = NZ * NX
    steps, _, width = w_query.shape
    span = x_any.shape[1]
    length = tokens.shape[0]
    each = HEADS // steps

    barrier = pltpu.get_barrier_semaphore()
    others = [(lax.rem(spot + k, spots), column_of) for k in range(1, spots)]
    others += [partner(CORE, z, x, y, c), partner(BY_Y, z, x, y, c)]
    for other in others:
        pl.semaphore_signal(
            barrier, inc=1, device_id=other, device_id_type=pl.DeviceIdType.MESH
        )

    def load(k, j):
        src = (query_any, key_any, value_any, w_out_any)[k]
        dst = (w_query, w_key, w_value, w_out)[k]
        cut = pl.ds(j * width, width)
        return pltpu.make_async_copy(
            src.at[cut] if k == 3 else src.at[:, cut], dst.at[j], weight_sem.at[k, j]
        )

    for j in range(steps):
        for k in range(4):
            load(k, j).start()
    mine = pl.ds(pl.multiple_of(spot * span, span), span)
    stay = pltpu.make_async_copy(x_any.at[spot], tokens.at[mine], stay_sem)
    stay.start()
    per_half = EXPERTS // NY
    lines, place_in = position_rows(crop_ref[...], y, per_half, length // 4)
    for k, value in enumerate(lines):
        info_ref[y, c, spot, k : k + 1, :] = value.astype(jnp.int32)
    info_ref[y, c, spot, len(lines) :, :] = jnp.zeros((8 - len(lines), length), jnp.int32)
    pl.semaphore_wait(barrier, spots + 1)

    def remote(src, dst, send, arrive, target):
        return pltpu.make_async_remote_copy(
            src_ref=src,
            dst_ref=dst,
            send_sem=send,
            recv_sem=arrive,
            device_id=target,
            device_id_type=pl.DeviceIdType.MESH,
        )

    for k in range(1, spots):
        there = lax.rem(spot + k, spots)
        remote(
            x_any.at[there], tokens.at[mine], x_sem.at[0], x_sem.at[1], (there, column_of)
        ).start()
    own_info = info_ref.at[y, c, spot]
    for k in range(1, spots):
        there = lax.rem(spot + k, spots)
        remote(own_info, own_info, info_sem.at[0], info_sem.at[1], (there, column_of)).start()

    until = lax.broadcasted_iota(jnp.int32, (length, length), 0) <= lax.broadcasted_iota(
        jnp.int32, (length, length), 1
    )
    running = jnp.dot(
        decay_ref[...],
        jnp.where(until, 1.0, 0.0),
        preferred_element_type=jnp.float32,
        precision=lax.Precision.HIGHEST,
    )
    padded[...] = jnp.zeros_like(padded)
    padded[:HEADS] = running
    upright = jnp.transpose(padded[...])
    head_gain = head_gain_ref[...].reshape(1, D).astype(jnp.float32)
    for j in range(steps):
        head_gain_rows[j] = head_gain[:, j * width : (j + 1) * width]
        line_ref[j] = running[j * each : (j + 1) * each]
        column_ref[j] = upright[:, j * each : (j + 1) * each]

    seven = tokens.at[pl.ds(0, (spots - 1) * span)]
    remote(seven, seven, x_sem.at[0], x_sem.at[1], others[0]).wait_recv()
    stay.wait()
    widened = tokens[...].astype(jnp.float32)
    scaled = widened * rms_scale(widened, 1e-05) * attn_gain_ref[...].reshape(1, D).astype(jnp.float32)
    normed[...] = scaled.astype(jnp.bfloat16)
    total_ref[...] = widened

    def core_pass():
        return remote(
            info_ref.at[y, c], info_ref.at[y, c], pass_sem.at[0, 0], pass_sem.at[1, 0],
            partner(CORE, z, x, y, c),
        )

    def y_pass():
        return remote(
            info_ref.at[y], info_ref.at[y], pass_sem.at[0, 1], pass_sem.at[1, 1],
            partner(BY_Y, z, x, y, c),
        )

    def one_step(j, carry):
        for k in range(4):
            load(k, j).wait()

        def project(ref):
            return jnp.dot(
                normed[...], ref[j], preferred_element_type=jnp.float32
            ).astype(jnp.bfloat16)

        heads = attend_heads(
            project(w_query),
            project(w_key),
            project(w_value),
            column_ref[j],
            line_ref[j],
            head_gain_rows[j],
        )
        total_ref[...] += jnp.dot(heads, w_out[j], preferred_element_type=jnp.float32)

        @pl.when(j == 0)
        def _():
            landed = info_ref.at[y, c, pl.ds(0, spots - 1)]
            remote(landed, landed, info_sem.at[0], info_sem.at[1], others[0]).wait_recv()
            core_pass().start()

        @pl.when(j == 2)
        def _():
            landed = info_ref.at[y, 1 - c]
            remote(landed, landed, pass_sem.at[0, 0], pass_sem.at[1, 0], others[-2]).wait_recv()
            y_pass().start()

        return carry

    lax.fori_loop(0, steps, one_step, 0)
    resid = total_ref[...].astype(jnp.bfloat16)
    resid_ref[...] = resid
    wide = resid.astype(jnp.float32)
    scaled = wide * rms_scale(wide, 1e-05) * moe_gain_ref[...].reshape(1, D).astype(jnp.float32)
    routed_ref[...] = jnp.dot(
        place_in, scaled.astype(jnp.bfloat16), preferred_element_type=jnp.float32
    ).astype(jnp.bfloat16)

    y_landed = info_ref.at[1 - y]
    remote(y_landed, y_landed, pass_sem.at[0, 1], pass_sem.at[1, 1], others[-1]).wait_recv()
    low_count = info_ref[:, :, :, 3:4, :].reshape(NY * NC * spots, length)
    need_ref[0, 0] = jnp.max(jnp.maximum(low_count, length - low_count))
    remote(seven, seven, x_sem.at[0], x_sem.at[1], others[0]).wait_send()
    sent = info_ref.at[y, c, pl.ds(0, spots - 1)]
    remote(sent, sent, info_sem.at[0], info_sem.at[1], others[0]).wait_send()
    core_pass().wait_send()
    y_pass().wait_send()


def attend_here(x_spans, crops, decay, attn_gain, head_gain, moe_gain, w_query, w_key, w_value, w_out):
    spots, span = x_spans.shape[0], x_spans.shape[1]
    length = spots * span
    steps = 6
    width = D // steps
    vmem = pl.BlockSpec(memory_space=pltpu.VMEM)
    any_space = pl.BlockSpec(memory_space=pl.ANY)
    dma = pltpu.SemaphoreType.DMA
    return pl.pallas_call(
        attend_here_kernel,
        out_shape=(
            jax.ShapeDtypeStruct((length, D), jnp.bfloat16),
            jax.ShapeDtypeStruct((length, D), jnp.bfloat16),
            jax.ShapeDtypeStruct((NY, NC, spots, 8, length), jnp.int32),
            jax.ShapeDtypeStruct((1, 1), jnp.int32),
        ),
        in_specs=[any_space] + [vmem] * 5 + [any_space] * 4,
        out_specs=(vmem, vmem, vmem, pl.BlockSpec(memory_space=pltpu.SMEM)),
        scratch_shapes=[
            pltpu.VMEM((length, D), jnp.bfloat16),
            pltpu.VMEM((length, D), jnp.bfloat16),
            pltpu.VMEM((length, D), jnp.float32),
            pltpu.VMEM((length, length), jnp.float32),
            pltpu.VMEM((steps, 1, width), jnp.float32),
            pltpu.VMEM((steps, HEADS // steps, length), jnp.float32),
            pltpu.VMEM((steps, length, HEADS // steps), jnp.float32),
            pltpu.VMEM((steps, D, width), jnp.bfloat16),
            pltpu.VMEM((steps, D, width), jnp.bfloat16),
            pltpu.VMEM((steps, D, width), jnp.bfloat16),
            pltpu.VMEM((steps, width, D), jnp.bfloat16),
            dma((4, steps)),
            dma,
            dma((2,)),
            dma((2,)),
            dma((2, 2)),
        ],
        compiler_params=pltpu.CompilerParams(
            collective_id=0, has_side_effects=True, vmem_limit_bytes=60 * 1024 * 1024
        ),
    )(x_spans, crops, decay, attn_gain, head_gain, moe_gain, w_query, w_key, w_value, w_out)


def order_of(i, z):
    nearer = z + 1 - 2 * (z % 2)
    far = jnp.where(z < 2, 2, 1)
    last = jnp.where(z < 2, 3, 0)
    return jnp.where(i == 0, z, jnp.where(i == 1, nearer, jnp.where(i == 2, far, last)))


def experts_kernel(
    kept,
    info_ref,
    routed_ref,
    resid_ref,
    w_gate_any,
    w_up_any,
    w_down_any,
    out_ref,
    tokens,
    w_gate,
    w_up,
    w_down,
    packed,
    terms,
    core_buf,
    e_buf,
    x_buf,
    up_buf,
    down_buf,
    full,
    weight_sem,
    send_sem,
    core_send,
    base_arrive,
    extra_arrive,
    core_arrive,
    term_sem,
    e_send,
    e_arrive,
    x_send,
    x_arrive,
    chain_sem,
    full_sem,
):
    z, x, y, c = place()
    length = routed_ref.shape[0]
    half = length // 2
    extra = kept - half
    experts, _, width = w_gate.shape
    capacity = length // 4
    held = experts * capacity
    first_slot = (y * NC + c) * held
    mine, beside = chip_of(z, x, y), chip_of(z, x, 1 - y)
    base, more, whole = pl.ds(0, half), pl.ds(half, extra), pl.ds(0, kept)

    loads = [
        pltpu.make_async_copy(src, dst, weight_sem.at[k])
        for k, (src, dst) in enumerate(
            ((w_gate_any, w_gate), (w_up_any, w_up), (w_down_any, w_down))
        )
    ]
    for load in loads:
        load.start()
    tokens[c, mine] = routed_ref[...]
    greet(z, x, y, c)

    def remote(src, dst, send, arrive, kind):
        return pltpu.make_async_remote_copy(
            src_ref=src,
            dst_ref=dst,
            send_sem=send,
            recv_sem=arrive,
            device_id=partner(kind, z, x, y, c),
            device_id_type=pl.DeviceIdType.MESH,
        )

    def landed(block, arrive):
        remote(block, block, arrive, arrive, CORE).wait_recv()

    def left(block, sent):
        remote(block, block, sent, sent, CORE).wait_send()

    def base_to(kind, chip):
        block = tokens.at[c, chip, base]
        only_if(
            exists(kind, z),
            lambda: remote(block, block, send_sem.at[kind], base_arrive.at[chip], kind).start(),
        )

    def extra_to(chip):
        remote(
            tokens.at[c, chip, pl.ds(0, extra)],
            tokens.at[c, chip, more],
            send_sem.at[BY_Y],
            extra_arrive.at[chip],
            BY_Y,
        ).start()

    def to_core(bz, chip, part):
        block = tokens.at[c, chip, part]
        remote(block, block, core_send.at[bz], core_arrive.at[bz], CORE).start()

    def base_in(chip):
        landed(tokens.at[c, chip, base], base_arrive.at[chip])

    def spots(distance, body):
        if isinstance(distance, int) and distance == 0:
            body(z, None)
            return
        for sign, way in ((-1, Z_UP), (1, Z_DOWN)):
            bz = z + sign * distance
            inside = jnp.logical_and(bz >= 0, bz < NZ)
            pl.when(inside)(lambda bz=bz, way=way: body(bz, way))

    def along_z(distance, by):
        def body(bz, way):
            chip = chip_of(bz, x, by)
            base_in(chip)
            base_to(way, chip)
            base_to(BY_X, chip)
            extra_to(chip)
            to_core(bz, chip, base)

        spots(distance, body)

    def across_x(distance, by):
        def body(bz, _):
            chip = chip_of(bz, 1 - x, by)
            base_in(chip)
            extra_to(chip)
            to_core(bz, chip, base)

        spots(distance, body)

    def extras(distance):
        def body(bz, _):
            for bx, by in ((x, 1 - y), (x, y), (1 - x, y), (1 - x, 1 - y)):
                if isinstance(distance, int) and distance == 0 and bx is x and by is y:
                    continue
                chip = chip_of(bz, bx, by)
                landed(tokens.at[c, chip, more], extra_arrive.at[chip])
                to_core(bz, chip, more)

        spots(distance, body)

    def core_wait(bz):
        landed(tokens.at[1 - c, pl.ds(bz * LAYER, LAYER), whole], core_arrive.at[bz])

    slots = lax.broadcasted_iota(jnp.int32, (held, length), 0) + first_slot

    def select(bz, bx, by, core):
        hit = slots == info_ref[by, core, bz * NX + bx, pl.ds(y, 1), :]
        return jnp.where(hit, 1.0, 0.0).astype(jnp.bfloat16)[:, :kept]

    spread_over = [(bx, by) for bx in range(NX) for by in range(NY)]

    def pack(bz, core):
        for k, (bx, by) in enumerate(spread_over):
            picked = jnp.dot(
                select(bz, bx, by, core),
                tokens[core, chip_of(bz, bx, by), :kept],
                preferred_element_type=jnp.float32,
            ).astype(jnp.bfloat16)
            for j in range(experts):
                packed[j, core * LAYER + k] = picked[j * capacity : (j + 1) * capacity]

    def run_expert(j):
        given = packed[j].reshape(NC * LAYER * capacity, D)
        gate_act = jnp.dot(given, w_gate[j], preferred_element_type=jnp.float32)
        up_act = jnp.dot(given, w_up[j], preferred_element_type=jnp.float32)
        hidden = (gate_act / (1.0 + jnp.exp(-gate_act)) * up_act).astype(jnp.bfloat16)
        packed[j] = (
            jnp.dot(hidden, w_down[j], preferred_element_type=jnp.float32)
            .astype(jnp.bfloat16)
            .reshape(NC * LAYER, capacity, D)
        )

    def unpack(bz, core):
        for k, (bx, by) in enumerate(spread_over):
            term = jnp.concatenate(
                [packed[j, core * LAYER + k] for j in range(experts)], axis=0
            )
            terms[core, chip_of(bz, bx, by), :kept] = lax.dot_general(
                select(bz, bx, by, core),
                term,
                (((0,), (0,)), ((), ())),
                preferred_element_type=jnp.float32,
            ).astype(jnp.bfloat16)

    def term_copy(bz):
        layer = pl.ds(bz * LAYER, LAYER)
        return remote(
            terms.at[1 - c, layer, whole],
            core_buf.at[layer, whole],
            term_sem.at[0, bz],
            term_sem.at[1, bz],
            CORE,
        )

    def wide(ref, *index):
        return ref[index].astype(jnp.float32)

    def edges(bz):
        term_copy(bz).wait_recv()
        for bx, by in ((1 - x, 0), (1 - x, 1), (x, 0), (x, 1)):
            chip = chip_of(bz, bx, by)
            total = wide(core_buf, chip, more) + wide(terms, c, chip, more)
            core_buf[chip, more] = total.astype(jnp.bfloat16)
            remote(
                core_buf.at[chip, more], e_buf.at[chip], e_send, e_arrive.at[chip], BY_Y
            ).start()

    def planes(bz):
        for bx in (1 - x, x):
            for by in range(NY):
                chip = chip_of(bz, bx, by)
                landed(e_buf.at[chip], e_arrive.at[chip])
                total = wide(core_buf, chip, base) + wide(terms, c, chip, base)
                near = total[:extra] + wide(e_buf, chip)
                core_buf[chip, pl.ds(0, extra)] = near.astype(jnp.bfloat16)
                if extra < half:
                    core_buf[chip, pl.ds(extra, half - extra)] = total[extra:].astype(jnp.bfloat16)
                if bx is not x:
                    remote(
                        core_buf.at[chip, base], x_buf.at[bz, by], x_send, x_arrive.at[bz, by], BY_X
                    ).start()

    def chain_copy(by, bz, kind):
        block = (up_buf if kind == Z_UP else down_buf).at[by, bz]
        return remote(
            block, block, chain_sem.at[0, kind, by, bz], chain_sem.at[1, kind, by, bz], kind
        )

    def in_plane(by, bz):
        landed(x_buf.at[bz, by], x_arrive.at[bz, by])
        return wide(core_buf, chip_of(bz, x, by), base) + wide(x_buf, bz, by)

    def along(bz):
        for by in range(NY):
            total = in_plane(by, bz)
            for buf, kind, goes, comes in (
                (up_buf, Z_UP, bz > z, z > 0),
                (down_buf, Z_DOWN, bz < z, z < NZ - 1),
            ):

                @pl.when(goes)
                def _(buf=buf, kind=kind, comes=comes):
                    @pl.when(comes)
                    def _():
                        chain_copy(by, bz, kind).wait_recv()
                        buf[by, bz] = (total + wide(buf, by, bz)).astype(jnp.bfloat16)

                    @pl.when(jnp.logical_not(comes))
                    def _():
                        buf[by, bz] = total.astype(jnp.bfloat16)

                    chain_copy(by, bz, kind).start()

    def finish(by, target):
        total = in_plane(by, z)

        @pl.when(z == 0)
        def _():
            chain_copy(by, z, Z_DOWN).wait_recv()
            target[...] = (total + wide(down_buf, by, z)).astype(jnp.bfloat16)

        @pl.when(z == NZ - 1)
        def _():
            chain_copy(by, z, Z_UP).wait_recv()
            target[...] = (total + wide(up_buf, by, z)).astype(jnp.bfloat16)

        @pl.when(jnp.logical_and(z > 0, z < NZ - 1))
        def _():
            chain_copy(by, z, Z_DOWN).wait_recv()
            chain_copy(by, z, Z_UP).wait_recv()
            both = wide(up_buf, by, z) + wide(down_buf, by, z)
            target[...] = (total + both).astype(jnp.bfloat16)

    remote(
        tokens.at[c, mine, pl.ds(half, half)],
        tokens.at[c, mine, base],
        send_sem.at[CORE],
        base_arrive.at[mine],
        BY_Y,
    ).start()
    for kind in (Z_UP, Z_DOWN, BY_X):
        base_to(kind, mine)
    extra_to(mine)
    to_core(z, mine, whole)
    base_in(beside)
    for kind in (Z_UP, Z_DOWN, BY_X):
        base_to(kind, beside)
    to_core(z, beside, base)
    along_z(1, y)
    across_x(0, y)
    along_z(1, 1 - y)
    across_x(0, 1 - y)
    extras(0)
    core_wait(z)
    for load in loads:
        load.wait()

    def step(i, carry):
        bz = order_of(i, z)
        before = order_of(i - 1, z)
        pack(bz, 0)
        pack(bz, 1)

        @pl.when(i == NZ - 1)
        def _():
            edges(before)

        run_expert(0)

        @pl.when(i < 2)
        def _():
            along_z(i + 2, y)

        run_expert(1)

        @pl.when(i < 3)
        def _():
            across_x(i + 1, y)

        unpack(bz, 1 - c)
        term_copy(bz).start()

        @pl.when(i == NZ - 1)
        def _():
            planes(before)

        unpack(bz, c)

        @pl.when(i < 2)
        def _():
            along_z(i + 2, 1 - y)

        @pl.when(i < 3)
        def _():
            across_x(i + 1, 1 - y)
            extras(i + 1)
            core_wait(order_of(i + 1, z))

        return carry

    lax.fori_loop(0, NZ, step, 0)
    far, farthest, nearer = order_of(2, z), order_of(3, z), order_of(1, z)
    edges(farthest)
    edges(nearer)
    along(far)
    planes(farthest)
    edges(z)
    planes(nearer)
    along(farthest)
    planes(z)
    along(nearer)
    given = core_buf.at[beside, base]
    finish(1 - y, given)
    give = remote(
        given, full.at[pl.ds(half, half)], full_sem.at[0], full_sem.at[1], BY_Y
    )
    give.start()
    finish(y, full.at[base])
    own_row = info_ref[y, c, z * NX + x, 2:3, :]
    rows = lax.broadcasted_iota(jnp.int32, (length, length), 0)
    place_in = jnp.where(rows == own_row, 1.0, 0.0).astype(jnp.bfloat16)
    landed(full.at[pl.ds(half, half)], full_sem.at[1])
    expert_out = lax.dot_general(
        place_in, full[...], (((0,), (0,)), ((), ())), preferred_element_type=jnp.float32
    )
    out_ref[...] = (resid_ref[...].astype(jnp.float32) + expert_out).astype(jnp.bfloat16)

    left(tokens.at[0, 0, base], send_sem.at[CORE])
    left(e_buf.at[pl.ds(0, CHIPS - 1)], send_sem.at[BY_Y])
    left(tokens.at[0, pl.ds(0, NZ)], send_sem.at[BY_X])
    for count in range(1, NZ):
        pl.when(z == count - 1)(
            lambda count=count: left(tokens.at[0, pl.ds(0, count)], send_sem.at[Z_UP])
        )
        pl.when(z == NZ - count)(
            lambda count=count: left(tokens.at[0, pl.ds(0, count)], send_sem.at[Z_DOWN])
        )
    left(e_buf, e_send)
    left(x_buf, x_send)
    left(given, full_sem.at[0])
    for bz in range(NZ):
        layer = pl.ds(bz * LAYER, LAYER)
        left(tokens.at[0, layer, whole], core_send.at[bz])
        left(terms.at[0, layer, whole], term_sem.at[0, bz])
        for by in range(NY):
            for kind, goes in ((Z_UP, bz > z), (Z_DOWN, bz < z)):
                pl.when(goes)(
                    lambda by=by, bz=bz, kind=kind: left(
                        up_buf.at[by, bz], chain_sem.at[0, kind, by, bz]
                    )
                )


def routed_experts(kept, number, info, routed, resid, w_gate, w_up, w_down):
    length = routed.shape[0]
    capacity = length // 4
    half = length // 2
    local_count, _, width = w_gate.shape

    def vmem(*shape):
        return pltpu.VMEM(shape, jnp.bfloat16)

    dma = pltpu.SemaphoreType.DMA
    any_space = pl.BlockSpec(memory_space=pl.ANY)
    in_vmem = pl.BlockSpec(memory_space=pltpu.VMEM)
    return pl.pallas_call(
        functools.partial(experts_kernel, kept),
        out_shape=jax.ShapeDtypeStruct((length, D), jnp.bfloat16),
        in_specs=[in_vmem, in_vmem, in_vmem, any_space, any_space, any_space],
        out_specs=in_vmem,
        scratch_shapes=[
            vmem(NC, CHIPS, length, D),
            vmem(local_count, D, width),
            vmem(local_count, D, width),
            vmem(local_count, width, D),
            vmem(local_count, NC * LAYER, capacity, D),
            vmem(NC, CHIPS, length, D),
            vmem(CHIPS, length, D),
            vmem(CHIPS, kept - half, D),
            vmem(NZ, NY, half, D),
            vmem(NY, NZ, half, D),
            vmem(NY, NZ, half, D),
            vmem(length, D),
            dma((3,)),
            dma((5,)),
            dma((NZ,)),
            dma((CHIPS,)),
            dma((CHIPS,)),
            dma((NZ,)),
            dma((2, NZ)),
            dma,
            dma((CHIPS,)),
            dma,
            dma((NZ, NY)),
            dma((2, 2, NY, NZ)),
            dma((2,)),
        ],
        compiler_params=pltpu.CompilerParams(
            collective_id=number, has_side_effects=True, vmem_limit_bytes=60 * 1024 * 1024
        ),
    )(info, routed, resid, w_gate, w_up, w_down)


def here(x_spans, crops, decay, attn_gain, head_gain, moe_gain, w_query, w_key, w_value, w_out, w_gate, w_up, w_down):
    span = x_spans.shape[3]
    length = x_spans.shape[1] * span
    resid, routed, info, need = attend_here(
        x_spans.reshape(-1, span, D),
        crops.reshape(1, length),
        decay.reshape(length, HEADS).T,
        attn_gain,
        head_gain,
        moe_gain,
        w_query,
        w_key,
        w_value,
        w_out,
    )
    operands = (info, routed, resid, w_gate, w_up, w_down)
    return lax.cond(
        need[0, 0] <= length * 3 // 4,
        functools.partial(routed_experts, length * 3 // 4, 1),
        functools.partial(routed_experts, length, 2),
        *operands,
    ).reshape(1, 1, length, D)


def on_device(
    x_spans,
    crops,
    decay,
    attn_gain,
    w_query,
    w_key,
    w_value,
    head_gain,
    w_out,
    moe_gain,
    w_gate,
    w_up,
    w_down,
):
    if lax.axis_size("dp") == NZ * NX and lax.axis_size("expert") == NY * NC:
        return here(
            x_spans,
            crops,
            decay,
            attn_gain,
            head_gain,
            moe_gain,
            w_query,
            w_key,
            w_value,
            w_out,
            w_gate,
            w_up,
            w_down,
        )
    arrived = lax.all_to_all(x_spans, "dp", split_axis=1, concat_axis=0, tiled=True)
    length = arrived.shape[0] * arrived.shape[3]
    tokens = arrived.reshape(length, D)
    forget = decay.reshape(length, HEADS)
    crop_ids = crops.reshape(length)
    capacity = length // 4
    position = slot_positions(crop_ids, capacity)
    resid, routed = attend(
        tokens, forget, attn_gain, w_query, w_key, w_value, head_gain, w_out, moe_gain
    )
    resid_wide = resid.astype(jnp.float32)
    select = (jnp.arange(EXPERTS * capacity, dtype=jnp.int32)[:, None] == position[None, :]).astype(
        jnp.bfloat16
    )
    packed = jnp.dot(select, routed, preferred_element_type=jnp.float32).astype(jnp.bfloat16)
    owners = lax.axis_size("expert")
    local_count = w_gate.shape[0]
    outgoing = packed.reshape(1, owners, EXPERTS * capacity // owners, D)
    gathered = spread(deliver(outgoing))
    sources = gathered.shape[0]
    grouped = gathered.reshape(sources, owners, local_count, capacity, D)
    gate_act = jnp.einsum("sojcd,jdf->sojcf", grouped, w_gate, preferred_element_type=jnp.float32)
    up_act = jnp.einsum("sojcd,jdf->sojcf", grouped, w_up, preferred_element_type=jnp.float32)
    hidden = (jax.nn.silu(gate_act) * up_act).astype(jnp.bfloat16)
    term = jnp.einsum("sojcf,jfd->sojcd", hidden, w_down, preferred_element_type=jnp.float32)
    summed = lax.psum_scatter(
        term.reshape(1 * lax.axis_size("dp"), owners, local_count * capacity, D).astype(
            jnp.bfloat16
        ),
        "dp",
        scatter_dimension=0,
        tiled=True,
    )
    own_sums = summed[0]
    returned = lax.all_to_all(own_sums, "expert", split_axis=0, concat_axis=0, tiled=True)
    flat_back = returned.reshape(EXPERTS * capacity, D)
    expert_out = jnp.einsum("pl,pd->ld", select, flat_back, preferred_element_type=jnp.float32)
    layer_sum = (resid_wide + expert_out).astype(jnp.bfloat16)
    return layer_sum.reshape(1, 1, length, D)


def solution(mesh):
    return jax.shard_map(
        on_device,
        mesh=mesh,
        in_specs=(
            P("dp", None, "expert", None, None),
            P("dp", "expert", None, None),
            P("dp", "expert", None, None),
            P(),
            P(),
            P(),
            P(),
            P(),
            P(),
            P(),
            P("expert", None, "dp"),
            P("expert", None, "dp"),
            P("expert", "dp", None),
        ),
        out_specs=P("dp", "expert", None, None),
        check_vma=False,
    )
```

```python
import functools

import jax
import jax.numpy as jnp
from jax import lax
from jax.experimental import pallas as pl
from jax.experimental.pallas import tpu as pltpu
from jax.sharding import PartitionSpec as P

D = 1536
HEADS = 24
HEAD_DIM = 64
EXPERTS = 8
LAYER = 4
NZ = 4
NX = 2
NY = 2
NC = 2
CHIPS = NZ * NX * NY
Z_UP, Z_DOWN, BY_X, BY_Y, CORE = range(5)


def place():
    dp, expert = lax.axis_index("dp"), lax.axis_index("expert")
    return dp // NX, dp % NX, expert // NC, expert % NC


def device(z, x, y, c):
    return (z * NX + x, y * NC + c)


def plot_of(z, x, y, c):
    return (z * NX + x) * (NY * NC) + y * NC + c


def chip_of(z, x, y):
    return (z * NX + x) * NY + y


def partner(kind, z, x, y, c):
    if kind == Z_UP:
        return device(z + 1, x, y, c)
    if kind == Z_DOWN:
        return device(z - 1, x, y, c)
    if kind == BY_X:
        return device(z, 1 - x, y, c)
    if kind == BY_Y:
        return device(z, x, 1 - y, c)
    return device(z, x, y, 1 - c)


def only_if(condition, body):
    if condition is None:
        body()
    else:
        pl.when(condition)(body)


def exists(kind, z):
    return {Z_UP: z < NZ - 1, Z_DOWN: z > 0}.get(kind)


def greet(z, x, y, c):
    barrier = pltpu.get_barrier_semaphore()
    for kind in range(5):

        def signal(kind=kind):
            pl.semaphore_signal(
                barrier,
                inc=1,
                device_id=partner(kind, z, x, y, c),
                device_id_type=pl.DeviceIdType.MESH,
            )

        only_if(exists(kind, z), signal)
    pl.semaphore_wait(barrier, 3 + jnp.where(z > 0, 1, 0) + jnp.where(z < NZ - 1, 1, 0))


def slot_positions(crop_ids, capacity):
    length = crop_ids.shape[0]
    same = crop_ids[:, None] == crop_ids[None, :]
    earlier = jnp.arange(length)[None, :] < jnp.arange(length)[:, None]
    slot_ids = jnp.sum(jnp.logical_and(same, earlier).astype(jnp.int32), axis=1)
    return crop_ids * capacity + slot_ids


def rms_scale(values, width_eps):
    return lax.rsqrt(jnp.mean(values * values, axis=-1, keepdims=True) + width_eps)


def spread(buffers):
    return lax.all_gather(buffers, "dp", axis=0, tiled=True)


def deliver(buffers):
    return lax.all_to_all(buffers, "expert", split_axis=1, concat_axis=1, tiled=True)


def attend_kernel(
    tokens_ref,
    column_ref,
    line_ref,
    attn_gain_ref,
    query_ref,
    key_ref,
    value_ref,
    head_gain_ref,
    w_out_ref,
    moe_gain_ref,
    resid_ref,
    routed_ref,
    normed_ref,
    total_ref,
):
    step = pl.program_id(0)
    length = tokens_ref.shape[0]

    @pl.when(step == 0)
    def _():
        widened = tokens_ref[...].astype(jnp.float32)
        scaled = widened * rms_scale(widened, 1e-05) * attn_gain_ref[...].astype(jnp.float32)
        normed_ref[...] = scaled.astype(jnp.bfloat16)
        total_ref[...] = widened

    def project(ref):
        return jnp.dot(
            normed_ref[...], ref[...], preferred_element_type=jnp.float32
        ).astype(jnp.bfloat16)

    query, key_vecs, value_vecs = project(query_ref), project(key_ref), project(value_ref)
    lanes = 2 * HEAD_DIM
    first = lax.broadcasted_iota(jnp.int32, (length, lanes), 1) < HEAD_DIM
    later = lax.broadcasted_iota(jnp.int32, (length, length), 0)
    causal = later >= lax.broadcasted_iota(jnp.int32, (length, length), 1)
    outcome = []
    for pair in range(query.shape[1] // lanes):
        cut = slice(pair * lanes, (pair + 1) * lanes)
        mixed = []
        for side in range(2):
            head = 2 * pair + side
            mask = first if side == 0 else jnp.logical_not(first)
            chosen = jnp.where(mask, query[:, cut], jnp.zeros((), jnp.bfloat16))
            scores = lax.dot_general(
                chosen,
                key_vecs[:, cut],
                (((1,), (1,)), ((), ())),
                preferred_element_type=jnp.float32,
            )
            gap = column_ref[0, :, head : head + 1] - line_ref[0, head : head + 1, :]
            weighted = scores * jnp.exp(jnp.where(causal, gap, -jnp.inf))
            coarse = weighted.astype(jnp.bfloat16)
            fine = (weighted - coarse.astype(jnp.float32)).astype(jnp.bfloat16)
            mixed.append(
                jnp.dot(coarse, value_vecs[:, cut], preferred_element_type=jnp.float32)
                + jnp.dot(fine, value_vecs[:, cut], preferred_element_type=jnp.float32)
            )
        both = jnp.where(first, mixed[0], mixed[1])
        square = both * both
        scale = [
            lax.rsqrt(
                jnp.sum(jnp.where(mask, square, 0.0), axis=-1, keepdims=True) / HEAD_DIM + 1e-05
            )
            for mask in (first, jnp.logical_not(first))
        ]
        gain = head_gain_ref[:, cut].astype(jnp.float32)
        outcome.append((both * jnp.where(first, scale[0], scale[1]) * gain).astype(jnp.bfloat16))
    total_ref[...] += jnp.dot(
        jnp.concatenate(outcome, axis=1), w_out_ref[...], preferred_element_type=jnp.float32
    )

    @pl.when(step == pl.num_programs(0) - 1)
    def _():
        resid = total_ref[...].astype(jnp.bfloat16)
        resid_ref[...] = resid
        wide = resid.astype(jnp.float32)
        scaled = wide * rms_scale(wide, 1e-05) * moe_gain_ref[...].astype(jnp.float32)
        routed_ref[...] = scaled.astype(jnp.bfloat16)


def attend(
    tokens, forget, attn_gain, w_query, w_key, w_value, head_gain, w_out, moe_gain
):
    length = tokens.shape[0]
    steps = 6
    width = D // steps
    until = jnp.arange(length)[None, :] <= jnp.arange(length)[:, None]
    cumulative = jnp.dot(until.astype(jnp.float32), forget, precision=lax.Precision.HIGHEST)
    line = cumulative.T.reshape(steps, HEADS // steps, length)
    column = jnp.transpose(line, (0, 2, 1))

    def whole(*shape):
        return pl.BlockSpec(shape, lambda j: (0,) * len(shape))

    columns = pl.BlockSpec((D, width), lambda j: (0, j))
    return pl.pallas_call(
        attend_kernel,
        grid=(steps,),
        out_shape=(
            jax.ShapeDtypeStruct((length, D), jnp.bfloat16),
            jax.ShapeDtypeStruct((length, D), jnp.bfloat16),
        ),
        in_specs=[
            whole(length, D),
            pl.BlockSpec((1, length, HEADS // steps), lambda j: (j, 0, 0)),
            pl.BlockSpec((1, HEADS // steps, length), lambda j: (j, 0, 0)),
            whole(1, D),
            columns,
            columns,
            columns,
            pl.BlockSpec((1, width), lambda j: (0, j)),
            pl.BlockSpec((width, D), lambda j: (j, 0)),
            whole(1, D),
        ],
        out_specs=(whole(length, D), whole(length, D)),
        scratch_shapes=[
            pltpu.VMEM((length, D), jnp.bfloat16),
            pltpu.VMEM((length, D), jnp.float32),
        ],
        compiler_params=pltpu.CompilerParams(vmem_limit_bytes=56 * 1024 * 1024),
    )(
        tokens,
        column,
        line,
        attn_gain.reshape(1, D),
        w_query,
        w_key,
        w_value,
        head_gain.reshape(1, D),
        w_out,
        moe_gain.reshape(1, D),
    )


def position_rows(crop, y, per_half, capacity):
    length = crop.shape[1]
    half = length // 2
    expert = lax.broadcasted_iota(jnp.int32, (EXPERTS, length), 0)
    hot = jnp.where(expert == crop, 1.0, 0.0)
    sooner = lax.broadcasted_iota(jnp.int32, (length, length), 0) < lax.broadcasted_iota(
        jnp.int32, (length, length), 1
    )
    ahead = jnp.dot(
        hot.astype(jnp.bfloat16),
        jnp.where(sooner, 1.0, 0.0).astype(jnp.bfloat16),
        preferred_element_type=jnp.float32,
    )
    slot = jnp.sum(hot * ahead, axis=0, keepdims=True)
    place_of = crop.astype(jnp.float32) * capacity + slot
    low_ahead = jnp.sum(jnp.where(expert < per_half, ahead, 0.0), axis=0, keepdims=True)
    low = crop < per_half
    low_count = jnp.sum(jnp.where(low, 1.0, 0.0), axis=1, keepdims=True)
    date = lax.broadcasted_iota(jnp.int32, (1, length), 1).astype(jnp.float32)
    rank = jnp.where(low, low_ahead, date - low_ahead)
    within = jnp.where(rank < half, half - 1 - rank, rank)
    crossed = jnp.where(within < half, within + half, within - half)
    row_for = (jnp.where(low, within, crossed), jnp.where(low, crossed, within))
    rows = lax.broadcasted_iota(jnp.int32, (length, length), 0).astype(jnp.float32)
    wide_place = jnp.broadcast_to(place_of, (EXPERTS, length)).astype(jnp.bfloat16)
    ordered = [
        lax.dot_general(
            wide_place,
            jnp.where(rows == row, 1.0, 0.0).astype(jnp.bfloat16),
            (((1,), (1,)), ((), ())),
            preferred_element_type=jnp.float32,
        )[:1]
        for row in row_for
    ]
    own_row = jnp.where(y == 0, row_for[0], row_for[1])
    count = jnp.broadcast_to(low_count, (1, length))
    lines = (ordered[0], ordered[1], own_row, count)
    place_in = jnp.where(rows == own_row, 1.0, 0.0).astype(jnp.bfloat16)
    return lines, place_in


def attend_heads(query, key_vecs, value_vecs, column, line, gain):
    length = query.shape[0]
    lanes = 2 * HEAD_DIM
    first = lax.broadcasted_iota(jnp.int32, (length, lanes), 1) < HEAD_DIM
    later = lax.broadcasted_iota(jnp.int32, (length, length), 0)
    causal = later >= lax.broadcasted_iota(jnp.int32, (length, length), 1)
    none = jnp.zeros((), jnp.bfloat16)
    outcome = []
    for pair in range(query.shape[1] // lanes):
        cut = slice(pair * lanes, (pair + 1) * lanes)
        chosen = query[:, cut]
        both_heads = jnp.concatenate(
            [jnp.where(first, chosen, none), jnp.where(first, none, chosen)], axis=0
        )
        scores = lax.dot_general(
            both_heads, key_vecs[:, cut], (((1,), (1,)), ((), ())), preferred_element_type=jnp.float32
        )
        weighted = []
        for side in range(2):
            head = 2 * pair + side
            gap = column[:, head : head + 1] - line[head : head + 1, :]
            fade = jnp.exp(jnp.where(causal, gap, -jnp.inf))
            weighted.append(
                (scores[side * length : (side + 1) * length] * fade).astype(jnp.bfloat16)
            )
        mixed = jnp.dot(
            jnp.concatenate(weighted, axis=0), value_vecs[:, cut], preferred_element_type=jnp.float32
        )
        both = jnp.where(first, mixed[:length], mixed[length:])
        square = both * both
        scale = [
            lax.rsqrt(jnp.sum(part, axis=-1, keepdims=True) / HEAD_DIM + 1e-05)
            for part in (jnp.where(first, square, 0.0), jnp.where(first, 0.0, square))
        ]
        outcome.append((both * jnp.where(first, scale[0], scale[1]) * gain[:, cut]).astype(jnp.bfloat16))
    return jnp.concatenate(outcome, axis=1)


def attend_here_kernel(
    x_any,
    crop_ref,
    decay_ref,
    attn_gain_ref,
    head_gain_ref,
    moe_gain_ref,
    query_any,
    key_any,
    value_any,
    w_out_any,
    resid_ref,
    routed_ref,
    info_ref,
    need_ref,
    tokens,
    normed,
    total_ref,
    padded,
    head_gain_rows,
    line_ref,
    column_ref,
    w_query,
    w_key,
    w_value,
    w_out,
    weight_sem,
    stay_sem,
    x_sem,
    info_sem,
    pass_sem,
):
    z, x, y, c = place()
    spot, column_of = z * NX + x, y * NC + c
    spots = NZ * NX
    steps, _, width = w_query.shape
    span = x_any.shape[1]
    length = tokens.shape[0]
    each = HEADS // steps

    barrier = pltpu.get_barrier_semaphore()
    others = [(lax.rem(spot + k, spots), column_of) for k in range(1, spots)]
    others += [partner(CORE, z, x, y, c), partner(BY_Y, z, x, y, c)]
    for other in others:
        pl.semaphore_signal(
            barrier, inc=1, device_id=other, device_id_type=pl.DeviceIdType.MESH
        )

    def load(k, j):
        src = (query_any, key_any, value_any, w_out_any)[k]
        dst = (w_query, w_key, w_value, w_out)[k]
        cut = pl.ds(j * width, width)
        return pltpu.make_async_copy(
            src.at[cut] if k == 3 else src.at[:, cut], dst.at[j], weight_sem.at[k, j]
        )

    for j in range(steps):
        for k in range(4):
            load(k, j).start()
    mine = pl.ds(pl.multiple_of(spot * span, span), span)
    stay = pltpu.make_async_copy(x_any.at[spot], tokens.at[mine], stay_sem)
    stay.start()
    per_half = EXPERTS // NY
    lines, place_in = position_rows(crop_ref[...], y, per_half, length // 4)
    for k, value in enumerate(lines):
        info_ref[y, c, spot, k : k + 1, :] = value.astype(jnp.int32)
    info_ref[y, c, spot, len(lines) :, :] = jnp.zeros((8 - len(lines), length), jnp.int32)
    pl.semaphore_wait(barrier, spots + 1)

    def remote(src, dst, send, arrive, target):
        return pltpu.make_async_remote_copy(
            src_ref=src,
            dst_ref=dst,
            send_sem=send,
            recv_sem=arrive,
            device_id=target,
            device_id_type=pl.DeviceIdType.MESH,
        )

    own_info = info_ref.at[y, c, spot]
    for k in range(1, spots):
        there = lax.rem(spot + k, spots)
        remote(own_info, own_info, info_sem.at[0], info_sem.at[1], (there, column_of)).start()
    for k in range(1, spots):
        there = lax.rem(spot + k, spots)
        remote(
            x_any.at[there], tokens.at[mine], x_sem.at[0], x_sem.at[1], (there, column_of)
        ).start()

    until = lax.broadcasted_iota(jnp.int32, (length, length), 0) <= lax.broadcasted_iota(
        jnp.int32, (length, length), 1
    )
    running = jnp.dot(
        decay_ref[...],
        jnp.where(until, 1.0, 0.0),
        preferred_element_type=jnp.float32,
        precision=lax.Precision.HIGHEST,
    )
    padded[...] = jnp.zeros_like(padded)
    padded[:HEADS] = running
    upright = jnp.transpose(padded[...])
    head_gain = head_gain_ref[...].reshape(1, D).astype(jnp.float32)
    for j in range(steps):
        head_gain_rows[j] = head_gain[:, j * width : (j + 1) * width]
        line_ref[j] = running[j * each : (j + 1) * each]
        column_ref[j] = upright[:, j * each : (j + 1) * each]

    def core_pass():
        return remote(
            info_ref.at[y, c], info_ref.at[y, c], pass_sem.at[0, 0], pass_sem.at[1, 0],
            partner(CORE, z, x, y, c),
        )

    def y_pass():
        return remote(
            info_ref.at[y], info_ref.at[y], pass_sem.at[0, 1], pass_sem.at[1, 1],
            partner(BY_Y, z, x, y, c),
        )

    came = info_ref.at[y, c, pl.ds(0, spots - 1)]
    remote(came, came, info_sem.at[0], info_sem.at[1], others[0]).wait_recv()
    core_pass().start()
    seven = tokens.at[pl.ds(0, (spots - 1) * span)]
    remote(seven, seven, x_sem.at[0], x_sem.at[1], others[0]).wait_recv()
    stay.wait()
    widened = tokens[...].astype(jnp.float32)
    scaled = widened * rms_scale(widened, 1e-05) * attn_gain_ref[...].reshape(1, D).astype(jnp.float32)
    normed[...] = scaled.astype(jnp.bfloat16)
    total_ref[...] = widened

    def one_step(j, carry):
        for k in range(4):
            load(k, j).wait()

        def project(ref):
            return jnp.dot(
                normed[...], ref[j], preferred_element_type=jnp.float32
            ).astype(jnp.bfloat16)

        heads = attend_heads(
            project(w_query),
            project(w_key),
            project(w_value),
            column_ref[j],
            line_ref[j],
            head_gain_rows[j],
        )
        total_ref[...] += jnp.dot(heads, w_out[j], preferred_element_type=jnp.float32)

        @pl.when(j == 0)
        def _():
            landed = info_ref.at[y, 1 - c]
            remote(landed, landed, pass_sem.at[0, 0], pass_sem.at[1, 0], others[-2]).wait_recv()
            y_pass().start()

        return carry

    lax.fori_loop(0, steps, one_step, 0)
    resid = total_ref[...].astype(jnp.bfloat16)
    resid_ref[...] = resid
    wide = resid.astype(jnp.float32)
    scaled = wide * rms_scale(wide, 1e-05) * moe_gain_ref[...].reshape(1, D).astype(jnp.float32)
    routed_ref[...] = jnp.dot(
        place_in, scaled.astype(jnp.bfloat16), preferred_element_type=jnp.float32
    ).astype(jnp.bfloat16)

    y_landed = info_ref.at[1 - y]
    remote(y_landed, y_landed, pass_sem.at[0, 1], pass_sem.at[1, 1], others[-1]).wait_recv()
    low_count = info_ref[:, :, :, 3:4, :].reshape(NY * NC * spots, length)
    need_ref[0, 0] = jnp.max(jnp.maximum(low_count, length - low_count))
    remote(seven, seven, x_sem.at[0], x_sem.at[1], others[0]).wait_send()
    sent = info_ref.at[y, c, pl.ds(0, spots - 1)]
    remote(sent, sent, info_sem.at[0], info_sem.at[1], others[0]).wait_send()
    core_pass().wait_send()
    y_pass().wait_send()


def attend_here(x_spans, crops, decay, attn_gain, head_gain, moe_gain, w_query, w_key, w_value, w_out):
    spots, span = x_spans.shape[0], x_spans.shape[1]
    length = spots * span
    steps = 6
    width = D // steps
    vmem = pl.BlockSpec(memory_space=pltpu.VMEM)
    any_space = pl.BlockSpec(memory_space=pl.ANY)
    dma = pltpu.SemaphoreType.DMA
    return pl.pallas_call(
        attend_here_kernel,
        out_shape=(
            jax.ShapeDtypeStruct((length, D), jnp.bfloat16),
            jax.ShapeDtypeStruct((length, D), jnp.bfloat16),
            jax.ShapeDtypeStruct((NY, NC, spots, 8, length), jnp.int32),
            jax.ShapeDtypeStruct((1, 1), jnp.int32),
        ),
        in_specs=[any_space] + [vmem] * 5 + [any_space] * 4,
        out_specs=(vmem, vmem, vmem, pl.BlockSpec(memory_space=pltpu.SMEM)),
        scratch_shapes=[
            pltpu.VMEM((length, D), jnp.bfloat16),
            pltpu.VMEM((length, D), jnp.bfloat16),
            pltpu.VMEM((length, D), jnp.float32),
            pltpu.VMEM((length, length), jnp.float32),
            pltpu.VMEM((steps, 1, width), jnp.float32),
            pltpu.VMEM((steps, HEADS // steps, length), jnp.float32),
            pltpu.VMEM((steps, length, HEADS // steps), jnp.float32),
            pltpu.VMEM((steps, D, width), jnp.bfloat16),
            pltpu.VMEM((steps, D, width), jnp.bfloat16),
            pltpu.VMEM((steps, D, width), jnp.bfloat16),
            pltpu.VMEM((steps, width, D), jnp.bfloat16),
            dma((4, steps)),
            dma,
            dma((2,)),
            dma((2,)),
            dma((2, 2)),
        ],
        compiler_params=pltpu.CompilerParams(
            collective_id=0, has_side_effects=True, vmem_limit_bytes=60 * 1024 * 1024
        ),
    )(x_spans, crops, decay, attn_gain, head_gain, moe_gain, w_query, w_key, w_value, w_out)


def order_of(i, z):
    nearer = z + 1 - 2 * (z % 2)
    far = jnp.where(z < 2, 2, 1)
    last = jnp.where(z < 2, 3, 0)
    return jnp.where(i == 0, z, jnp.where(i == 1, nearer, jnp.where(i == 2, far, last)))


def experts_kernel(
    kept,
    info_ref,
    routed_ref,
    resid_ref,
    w_gate_any,
    w_up_any,
    w_down_any,
    out_ref,
    tokens,
    w_gate,
    w_up,
    w_down,
    packed,
    terms,
    core_buf,
    e_buf,
    x_buf,
    up_buf,
    down_buf,
    full,
    weight_sem,
    send_sem,
    core_send,
    base_arrive,
    extra_arrive,
    core_arrive,
    term_sem,
    e_send,
    e_arrive,
    x_send,
    x_arrive,
    chain_sem,
    full_sem,
):
    z, x, y, c = place()
    length = routed_ref.shape[0]
    half = length // 2
    extra = kept - half
    experts, _, width = w_gate.shape
    capacity = length // 4
    held = experts * capacity
    first_slot = (y * NC + c) * held
    mine, beside = chip_of(z, x, y), chip_of(z, x, 1 - y)
    base, more, whole = pl.ds(0, half), pl.ds(half, extra), pl.ds(0, kept)

    loads = [
        pltpu.make_async_copy(src, dst, weight_sem.at[k])
        for k, (src, dst) in enumerate(
            ((w_gate_any, w_gate), (w_up_any, w_up), (w_down_any, w_down))
        )
    ]
    for load in loads:
        load.start()
    tokens[c, mine] = routed_ref[...]
    greet(z, x, y, c)

    def remote(src, dst, send, arrive, kind):
        return pltpu.make_async_remote_copy(
            src_ref=src,
            dst_ref=dst,
            send_sem=send,
            recv_sem=arrive,
            device_id=partner(kind, z, x, y, c),
            device_id_type=pl.DeviceIdType.MESH,
        )

    def landed(block, arrive):
        remote(block, block, arrive, arrive, CORE).wait_recv()

    def left(block, sent):
        remote(block, block, sent, sent, CORE).wait_send()

    def base_to(kind, chip):
        block = tokens.at[c, chip, base]
        only_if(
            exists(kind, z),
            lambda: remote(block, block, send_sem.at[kind], base_arrive.at[chip], kind).start(),
        )

    def extra_to(chip):
        remote(
            tokens.at[c, chip, pl.ds(0, extra)],
            tokens.at[c, chip, more],
            send_sem.at[BY_Y],
            extra_arrive.at[chip],
            BY_Y,
        ).start()

    def to_core(bz, chip, part):
        block = tokens.at[c, chip, part]
        remote(block, block, core_send.at[bz], core_arrive.at[bz], CORE).start()

    def base_in(chip):
        landed(tokens.at[c, chip, base], base_arrive.at[chip])

    def spots(distance, body):
        if isinstance(distance, int) and distance == 0:
            body(z, None)
            return
        for sign, way in ((-1, Z_UP), (1, Z_DOWN)):
            bz = z + sign * distance
            inside = jnp.logical_and(bz >= 0, bz < NZ)
            pl.when(inside)(lambda bz=bz, way=way: body(bz, way))

    def along_z(distance, by):
        def body(bz, way):
            chip = chip_of(bz, x, by)
            base_in(chip)
            base_to(way, chip)
            base_to(BY_X, chip)
            extra_to(chip)
            to_core(bz, chip, base)

        spots(distance, body)

    def across_x(distance, by):
        def body(bz, _):
            chip = chip_of(bz, 1 - x, by)
            base_in(chip)
            extra_to(chip)
            to_core(bz, chip, base)

        spots(distance, body)

    def extras(distance):
        def body(bz, _):
            for bx, by in ((x, 1 - y), (x, y), (1 - x, y), (1 - x, 1 - y)):
                if isinstance(distance, int) and distance == 0 and bx is x and by is y:
                    continue
                chip = chip_of(bz, bx, by)
                landed(tokens.at[c, chip, more], extra_arrive.at[chip])
                to_core(bz, chip, more)

        spots(distance, body)

    def core_wait(bz):
        landed(tokens.at[1 - c, pl.ds(bz * LAYER, LAYER), whole], core_arrive.at[bz])

    slots = lax.broadcasted_iota(jnp.int32, (held, length), 0) + first_slot

    def select(bz, bx, by, core):
        hit = slots == info_ref[by, core, bz * NX + bx, pl.ds(y, 1), :]
        return jnp.where(hit, 1.0, 0.0).astype(jnp.bfloat16)[:, :kept]

    spread_over = [(bx, by) for bx in range(NX) for by in range(NY)]

    def pack(bz, core):
        for k, (bx, by) in enumerate(spread_over):
            picked = jnp.dot(
                select(bz, bx, by, core),
                tokens[core, chip_of(bz, bx, by), :kept],
                preferred_element_type=jnp.float32,
            ).astype(jnp.bfloat16)
            for j in range(experts):
                packed[j, core * LAYER + k] = picked[j * capacity : (j + 1) * capacity]

    def run_expert(j):
        given = packed[j].reshape(NC * LAYER * capacity, D)
        gate_act = jnp.dot(given, w_gate[j], preferred_element_type=jnp.float32)
        up_act = jnp.dot(given, w_up[j], preferred_element_type=jnp.float32)
        hidden = (gate_act / (1.0 + jnp.exp(-gate_act)) * up_act).astype(jnp.bfloat16)
        packed[j] = (
            jnp.dot(hidden, w_down[j], preferred_element_type=jnp.float32)
            .astype(jnp.bfloat16)
            .reshape(NC * LAYER, capacity, D)
        )

    def unpack(bz, core):
        for k, (bx, by) in enumerate(spread_over):
            term = jnp.concatenate(
                [packed[j, core * LAYER + k] for j in range(experts)], axis=0
            )
            terms[core, chip_of(bz, bx, by), :kept] = lax.dot_general(
                select(bz, bx, by, core),
                term,
                (((0,), (0,)), ((), ())),
                preferred_element_type=jnp.float32,
            ).astype(jnp.bfloat16)

    def term_copy(bz):
        layer = pl.ds(bz * LAYER, LAYER)
        return remote(
            terms.at[1 - c, layer, whole],
            core_buf.at[layer, whole],
            term_sem.at[0, bz],
            term_sem.at[1, bz],
            CORE,
        )

    def wide(ref, *index):
        return ref[index].astype(jnp.float32)

    def edges(bz):
        term_copy(bz).wait_recv()
        for bx, by in ((1 - x, 1 - y), (1 - x, y), (x, 1 - y), (x, y)):
            chip = chip_of(bz, bx, by)
            total = wide(core_buf, chip, more) + wide(terms, c, chip, more)
            core_buf[chip, more] = total.astype(jnp.bfloat16)
            remote(
                core_buf.at[chip, more], e_buf.at[chip], e_send, e_arrive.at[chip], BY_Y
            ).start()

    def planes(bz):
        for bx in (1 - x, x):
            for by in (1 - y, y):
                chip = chip_of(bz, bx, by)
                landed(e_buf.at[chip], e_arrive.at[chip])
                total = wide(core_buf, chip, base) + wide(terms, c, chip, base)
                near = total[:extra] + wide(e_buf, chip)
                core_buf[chip, pl.ds(0, extra)] = near.astype(jnp.bfloat16)
                if extra < half:
                    core_buf[chip, pl.ds(extra, half - extra)] = total[extra:].astype(jnp.bfloat16)
                if bx is not x:
                    remote(
                        core_buf.at[chip, base], x_buf.at[bz, by], x_send, x_arrive.at[bz, by], BY_X
                    ).start()

    def chain_copy(by, bz, kind):
        block = (up_buf if kind == Z_UP else down_buf).at[by, bz]
        return remote(
            block, block, chain_sem.at[0, kind, by, bz], chain_sem.at[1, kind, by, bz], kind
        )

    def in_plane(by, bz):
        landed(x_buf.at[bz, by], x_arrive.at[bz, by])
        return wide(core_buf, chip_of(bz, x, by), base) + wide(x_buf, bz, by)

    def along(bz):
        for by in (1 - y, y):
            total = in_plane(by, bz)
            for buf, kind, goes, comes in (
                (up_buf, Z_UP, bz > z, z > 0),
                (down_buf, Z_DOWN, bz < z, z < NZ - 1),
            ):

                @pl.when(goes)
                def _(buf=buf, kind=kind, comes=comes):
                    @pl.when(comes)
                    def _():
                        chain_copy(by, bz, kind).wait_recv()
                        buf[by, bz] = (total + wide(buf, by, bz)).astype(jnp.bfloat16)

                    @pl.when(jnp.logical_not(comes))
                    def _():
                        buf[by, bz] = total.astype(jnp.bfloat16)

                    chain_copy(by, bz, kind).start()

    def finish(by, target):
        total = in_plane(by, z)

        @pl.when(z == 0)
        def _():
            chain_copy(by, z, Z_DOWN).wait_recv()
            target[...] = (total + wide(down_buf, by, z)).astype(jnp.bfloat16)

        @pl.when(z == NZ - 1)
        def _():
            chain_copy(by, z, Z_UP).wait_recv()
            target[...] = (total + wide(up_buf, by, z)).astype(jnp.bfloat16)

        @pl.when(jnp.logical_and(z > 0, z < NZ - 1))
        def _():
            chain_copy(by, z, Z_DOWN).wait_recv()
            chain_copy(by, z, Z_UP).wait_recv()
            both = wide(up_buf, by, z) + wide(down_buf, by, z)
            target[...] = (total + both).astype(jnp.bfloat16)

    remote(
        tokens.at[c, mine, pl.ds(half, half)],
        tokens.at[c, mine, base],
        send_sem.at[CORE],
        base_arrive.at[mine],
        BY_Y,
    ).start()
    for kind in (Z_UP, Z_DOWN, BY_X):
        base_to(kind, mine)
    extra_to(mine)
    to_core(z, mine, whole)
    base_in(beside)
    for kind in (Z_UP, Z_DOWN, BY_X):
        base_to(kind, beside)
    to_core(z, beside, base)
    along_z(1, y)
    across_x(0, y)
    along_z(1, 1 - y)
    across_x(0, 1 - y)
    extras(0)
    core_wait(z)
    for load in loads:
        load.wait()

    def step(i, carry):
        bz = order_of(i, z)
        before = order_of(i - 1, z)
        @pl.when(i < 2)
        def _():
            along_z(i + 2, y)

        @pl.when(i < 3)
        def _():
            across_x(i + 1, y)

        @pl.when(i < 2)
        def _():
            along_z(i + 2, 1 - y)

        pack(bz, 0)

        pack(bz, 1)

        @pl.when(i == NZ - 1)
        def _():
            edges(before)

        run_expert(0)

        @pl.when(i < 3)
        def _():
            across_x(i + 1, 1 - y)

        run_expert(1)

        unpack(bz, 1 - c)

        term_copy(bz).start()

        @pl.when(i == NZ - 1)
        def _():
            planes(before)

        unpack(bz, c)

        @pl.when(i < 3)
        def _():
            extras(i + 1)
            core_wait(order_of(i + 1, z))

        return carry

    lax.fori_loop(0, NZ, step, 0)
    far, farthest, nearer = order_of(2, z), order_of(3, z), order_of(1, z)
    edges(farthest)
    edges(nearer)
    planes(farthest)
    along(far)
    edges(z)
    planes(nearer)
    along(farthest)
    planes(z)
    along(nearer)
    given = core_buf.at[beside, base]
    finish(1 - y, given)
    give = remote(
        given, full.at[pl.ds(half, half)], full_sem.at[0], full_sem.at[1], BY_Y
    )
    give.start()
    finish(y, full.at[base])
    own_row = info_ref[y, c, z * NX + x, 2:3, :]
    rows = lax.broadcasted_iota(jnp.int32, (length, length), 0)
    place_in = jnp.where(rows == own_row, 1.0, 0.0).astype(jnp.bfloat16)
    landed(full.at[pl.ds(half, half)], full_sem.at[1])
    expert_out = lax.dot_general(
        place_in, full[...], (((0,), (0,)), ((), ())), preferred_element_type=jnp.float32
    )
    out_ref[...] = (resid_ref[...].astype(jnp.float32) + expert_out).astype(jnp.bfloat16)

    left(tokens.at[0, 0, base], send_sem.at[CORE])
    left(e_buf.at[pl.ds(0, CHIPS - 1)], send_sem.at[BY_Y])
    left(tokens.at[0, pl.ds(0, NZ)], send_sem.at[BY_X])
    for count in range(1, NZ):
        pl.when(z == count - 1)(
            lambda count=count: left(tokens.at[0, pl.ds(0, count)], send_sem.at[Z_UP])
        )
        pl.when(z == NZ - count)(
            lambda count=count: left(tokens.at[0, pl.ds(0, count)], send_sem.at[Z_DOWN])
        )
    left(e_buf, e_send)
    left(x_buf, x_send)
    left(given, full_sem.at[0])
    for bz in range(NZ):
        layer = pl.ds(bz * LAYER, LAYER)
        left(tokens.at[0, layer, whole], core_send.at[bz])
        left(terms.at[0, layer, whole], term_sem.at[0, bz])
        for by in range(NY):
            for kind, goes in ((Z_UP, bz > z), (Z_DOWN, bz < z)):
                pl.when(goes)(
                    lambda by=by, bz=bz, kind=kind: left(
                        up_buf.at[by, bz], chain_sem.at[0, kind, by, bz]
                    )
                )


def routed_experts(kept, number, info, routed, resid, w_gate, w_up, w_down):
    length = routed.shape[0]
    capacity = length // 4
    half = length // 2
    local_count, _, width = w_gate.shape

    def vmem(*shape):
        return pltpu.VMEM(shape, jnp.bfloat16)

    dma = pltpu.SemaphoreType.DMA
    any_space = pl.BlockSpec(memory_space=pl.ANY)
    in_vmem = pl.BlockSpec(memory_space=pltpu.VMEM)
    return pl.pallas_call(
        functools.partial(experts_kernel, kept),
        out_shape=jax.ShapeDtypeStruct((length, D), jnp.bfloat16),
        in_specs=[in_vmem, in_vmem, in_vmem, any_space, any_space, any_space],
        out_specs=in_vmem,
        scratch_shapes=[
            vmem(NC, CHIPS, length, D),
            vmem(local_count, D, width),
            vmem(local_count, D, width),
            vmem(local_count, width, D),
            vmem(local_count, NC * LAYER, capacity, D),
            vmem(NC, CHIPS, length, D),
            vmem(CHIPS, length, D),
            vmem(CHIPS, kept - half, D),
            vmem(NZ, NY, half, D),
            vmem(NY, NZ, half, D),
            vmem(NY, NZ, half, D),
            vmem(length, D),
            dma((3,)),
            dma((5,)),
            dma((NZ,)),
            dma((CHIPS,)),
            dma((CHIPS,)),
            dma((NZ,)),
            dma((2, NZ)),
            dma,
            dma((CHIPS,)),
            dma,
            dma((NZ, NY)),
            dma((2, 2, NY, NZ)),
            dma((2,)),
        ],
        compiler_params=pltpu.CompilerParams(
            collective_id=number, has_side_effects=True, vmem_limit_bytes=60 * 1024 * 1024
        ),
    )(info, routed, resid, w_gate, w_up, w_down)


def here(x_spans, crops, decay, attn_gain, head_gain, moe_gain, w_query, w_key, w_value, w_out, w_gate, w_up, w_down):
    span = x_spans.shape[3]
    length = x_spans.shape[1] * span
    resid, routed, info, need = attend_here(
        x_spans.reshape(-1, span, D),
        crops.reshape(1, length),
        decay.reshape(length, HEADS).T,
        attn_gain,
        head_gain,
        moe_gain,
        w_query,
        w_key,
        w_value,
        w_out,
    )
    operands = (info, routed, resid, w_gate, w_up, w_down)
    return lax.cond(
        need[0, 0] <= length * 3 // 4,
        functools.partial(routed_experts, length * 3 // 4, 1),
        functools.partial(routed_experts, length, 2),
        *operands,
    ).reshape(1, 1, length, D)


def on_device(
    x_spans,
    crops,
    decay,
    attn_gain,
    w_query,
    w_key,
    w_value,
    head_gain,
    w_out,
    moe_gain,
    w_gate,
    w_up,
    w_down,
):
    if lax.axis_size("dp") == NZ * NX and lax.axis_size("expert") == NY * NC:
        return here(
            x_spans,
            crops,
            decay,
            attn_gain,
            head_gain,
            moe_gain,
            w_query,
            w_key,
            w_value,
            w_out,
            w_gate,
            w_up,
            w_down,
        )
    arrived = lax.all_to_all(x_spans, "dp", split_axis=1, concat_axis=0, tiled=True)
    length = arrived.shape[0] * arrived.shape[3]
    tokens = arrived.reshape(length, D)
    forget = decay.reshape(length, HEADS)
    crop_ids = crops.reshape(length)
    capacity = length // 4
    position = slot_positions(crop_ids, capacity)
    resid, routed = attend(
        tokens, forget, attn_gain, w_query, w_key, w_value, head_gain, w_out, moe_gain
    )
    resid_wide = resid.astype(jnp.float32)
    select = (jnp.arange(EXPERTS * capacity, dtype=jnp.int32)[:, None] == position[None, :]).astype(
        jnp.bfloat16
    )
    packed = jnp.dot(select, routed, preferred_element_type=jnp.float32).astype(jnp.bfloat16)
    owners = lax.axis_size("expert")
    local_count = w_gate.shape[0]
    outgoing = packed.reshape(1, owners, EXPERTS * capacity // owners, D)
    gathered = spread(deliver(outgoing))
    sources = gathered.shape[0]
    grouped = gathered.reshape(sources, owners, local_count, capacity, D)
    gate_act = jnp.einsum("sojcd,jdf->sojcf", grouped, w_gate, preferred_element_type=jnp.float32)
    up_act = jnp.einsum("sojcd,jdf->sojcf", grouped, w_up, preferred_element_type=jnp.float32)
    hidden = (jax.nn.silu(gate_act) * up_act).astype(jnp.bfloat16)
    term = jnp.einsum("sojcf,jfd->sojcd", hidden, w_down, preferred_element_type=jnp.float32)
    summed = lax.psum_scatter(
        term.reshape(1 * lax.axis_size("dp"), owners, local_count * capacity, D).astype(
            jnp.bfloat16
        ),
        "dp",
        scatter_dimension=0,
        tiled=True,
    )
    own_sums = summed[0]
    returned = lax.all_to_all(own_sums, "expert", split_axis=0, concat_axis=0, tiled=True)
    flat_back = returned.reshape(EXPERTS * capacity, D)
    expert_out = jnp.einsum("pl,pd->ld", select, flat_back, preferred_element_type=jnp.float32)
    layer_sum = (resid_wide + expert_out).astype(jnp.bfloat16)
    return layer_sum.reshape(1, 1, length, D)


def solution(mesh):
    return jax.shard_map(
        on_device,
        mesh=mesh,
        in_specs=(
            P("dp", None, "expert", None, None),
            P("dp", "expert", None, None),
            P("dp", "expert", None, None),
            P(),
            P(),
            P(),
            P(),
            P(),
            P(),
            P(),
            P("expert", None, "dp"),
            P("expert", None, "dp"),
            P("expert", "dp", None),
        ),
        out_specs=P("dp", "expert", None, None),
        check_vma=False,
    )
```

```python
import functools

import jax
import jax.numpy as jnp
from jax import lax
from jax.experimental import pallas as pl
from jax.experimental.pallas import tpu as pltpu
from jax.sharding import PartitionSpec as P

D = 1536
HEADS = 24
HEAD_DIM = 64
EXPERTS = 8
LAYER = 4
NZ = 4
NX = 2
NY = 2
NC = 2
CHIPS = NZ * NX * NY
Z_UP, Z_DOWN, BY_X, BY_Y, CORE = range(5)


def place():
    dp, expert = lax.axis_index("dp"), lax.axis_index("expert")
    return dp // NX, dp % NX, expert // NC, expert % NC


def device(z, x, y, c):
    return (z * NX + x, y * NC + c)


def plot_of(z, x, y, c):
    return (z * NX + x) * (NY * NC) + y * NC + c


def chip_of(z, x, y):
    return (z * NX + x) * NY + y


def partner(kind, z, x, y, c):
    if kind == Z_UP:
        return device(z + 1, x, y, c)
    if kind == Z_DOWN:
        return device(z - 1, x, y, c)
    if kind == BY_X:
        return device(z, 1 - x, y, c)
    if kind == BY_Y:
        return device(z, x, 1 - y, c)
    return device(z, x, y, 1 - c)


def only_if(condition, body):
    if condition is None:
        body()
    else:
        pl.when(condition)(body)


def exists(kind, z):
    return {Z_UP: z < NZ - 1, Z_DOWN: z > 0}.get(kind)


def greet(z, x, y, c):
    barrier = pltpu.get_barrier_semaphore()
    for kind in range(5):

        def signal(kind=kind):
            pl.semaphore_signal(
                barrier,
                inc=1,
                device_id=partner(kind, z, x, y, c),
                device_id_type=pl.DeviceIdType.MESH,
            )

        only_if(exists(kind, z), signal)
    pl.semaphore_wait(barrier, 3 + jnp.where(z > 0, 1, 0) + jnp.where(z < NZ - 1, 1, 0))


def slot_positions(crop_ids, capacity):
    length = crop_ids.shape[0]
    same = crop_ids[:, None] == crop_ids[None, :]
    earlier = jnp.arange(length)[None, :] < jnp.arange(length)[:, None]
    slot_ids = jnp.sum(jnp.logical_and(same, earlier).astype(jnp.int32), axis=1)
    return crop_ids * capacity + slot_ids


def rms_scale(values, width_eps):
    return lax.rsqrt(jnp.mean(values * values, axis=-1, keepdims=True) + width_eps)


def spread(buffers):
    return lax.all_gather(buffers, "dp", axis=0, tiled=True)


def deliver(buffers):
    return lax.all_to_all(buffers, "expert", split_axis=1, concat_axis=1, tiled=True)


def attend_kernel(
    tokens_ref,
    column_ref,
    line_ref,
    attn_gain_ref,
    query_ref,
    key_ref,
    value_ref,
    head_gain_ref,
    w_out_ref,
    moe_gain_ref,
    resid_ref,
    routed_ref,
    normed_ref,
    total_ref,
):
    step = pl.program_id(0)
    length = tokens_ref.shape[0]

    @pl.when(step == 0)
    def _():
        widened = tokens_ref[...].astype(jnp.float32)
        scaled = widened * rms_scale(widened, 1e-05) * attn_gain_ref[...].astype(jnp.float32)
        normed_ref[...] = scaled.astype(jnp.bfloat16)
        total_ref[...] = widened

    def project(ref):
        return jnp.dot(
            normed_ref[...], ref[...], preferred_element_type=jnp.float32
        ).astype(jnp.bfloat16)

    query, key_vecs, value_vecs = project(query_ref), project(key_ref), project(value_ref)
    lanes = 2 * HEAD_DIM
    first = lax.broadcasted_iota(jnp.int32, (length, lanes), 1) < HEAD_DIM
    later = lax.broadcasted_iota(jnp.int32, (length, length), 0)
    causal = later >= lax.broadcasted_iota(jnp.int32, (length, length), 1)
    outcome = []
    for pair in range(query.shape[1] // lanes):
        cut = slice(pair * lanes, (pair + 1) * lanes)
        mixed = []
        for side in range(2):
            head = 2 * pair + side
            mask = first if side == 0 else jnp.logical_not(first)
            chosen = jnp.where(mask, query[:, cut], jnp.zeros((), jnp.bfloat16))
            scores = lax.dot_general(
                chosen,
                key_vecs[:, cut],
                (((1,), (1,)), ((), ())),
                preferred_element_type=jnp.float32,
            )
            gap = column_ref[0, :, head : head + 1] - line_ref[0, head : head + 1, :]
            weighted = scores * jnp.exp(jnp.where(causal, gap, -jnp.inf))
            coarse = weighted.astype(jnp.bfloat16)
            fine = (weighted - coarse.astype(jnp.float32)).astype(jnp.bfloat16)
            mixed.append(
                jnp.dot(coarse, value_vecs[:, cut], preferred_element_type=jnp.float32)
                + jnp.dot(fine, value_vecs[:, cut], preferred_element_type=jnp.float32)
            )
        both = jnp.where(first, mixed[0], mixed[1])
        square = both * both
        scale = [
            lax.rsqrt(
                jnp.sum(jnp.where(mask, square, 0.0), axis=-1, keepdims=True) / HEAD_DIM + 1e-05
            )
            for mask in (first, jnp.logical_not(first))
        ]
        gain = head_gain_ref[:, cut].astype(jnp.float32)
        outcome.append((both * jnp.where(first, scale[0], scale[1]) * gain).astype(jnp.bfloat16))
    total_ref[...] += jnp.dot(
        jnp.concatenate(outcome, axis=1), w_out_ref[...], preferred_element_type=jnp.float32
    )

    @pl.when(step == pl.num_programs(0) - 1)
    def _():
        resid = total_ref[...].astype(jnp.bfloat16)
        resid_ref[...] = resid
        wide = resid.astype(jnp.float32)
        scaled = wide * rms_scale(wide, 1e-05) * moe_gain_ref[...].astype(jnp.float32)
        routed_ref[...] = scaled.astype(jnp.bfloat16)


def attend(
    tokens, forget, attn_gain, w_query, w_key, w_value, head_gain, w_out, moe_gain
):
    length = tokens.shape[0]
    steps = 6
    width = D // steps
    until = jnp.arange(length)[None, :] <= jnp.arange(length)[:, None]
    cumulative = jnp.dot(until.astype(jnp.float32), forget, precision=lax.Precision.HIGHEST)
    line = cumulative.T.reshape(steps, HEADS // steps, length)
    column = jnp.transpose(line, (0, 2, 1))

    def whole(*shape):
        return pl.BlockSpec(shape, lambda j: (0,) * len(shape))

    columns = pl.BlockSpec((D, width), lambda j: (0, j))
    return pl.pallas_call(
        attend_kernel,
        grid=(steps,),
        out_shape=(
            jax.ShapeDtypeStruct((length, D), jnp.bfloat16),
            jax.ShapeDtypeStruct((length, D), jnp.bfloat16),
        ),
        in_specs=[
            whole(length, D),
            pl.BlockSpec((1, length, HEADS // steps), lambda j: (j, 0, 0)),
            pl.BlockSpec((1, HEADS // steps, length), lambda j: (j, 0, 0)),
            whole(1, D),
            columns,
            columns,
            columns,
            pl.BlockSpec((1, width), lambda j: (0, j)),
            pl.BlockSpec((width, D), lambda j: (j, 0)),
            whole(1, D),
        ],
        out_specs=(whole(length, D), whole(length, D)),
        scratch_shapes=[
            pltpu.VMEM((length, D), jnp.bfloat16),
            pltpu.VMEM((length, D), jnp.float32),
        ],
        compiler_params=pltpu.CompilerParams(vmem_limit_bytes=56 * 1024 * 1024),
    )(
        tokens,
        column,
        line,
        attn_gain.reshape(1, D),
        w_query,
        w_key,
        w_value,
        head_gain.reshape(1, D),
        w_out,
        moe_gain.reshape(1, D),
    )


def position_rows(crop, y, per_half, capacity):
    length = crop.shape[1]
    half = length // 2
    expert = lax.broadcasted_iota(jnp.int32, (EXPERTS, length), 0)
    hot = jnp.where(expert == crop, 1.0, 0.0)
    sooner = lax.broadcasted_iota(jnp.int32, (length, length), 0) < lax.broadcasted_iota(
        jnp.int32, (length, length), 1
    )
    ahead = jnp.dot(
        hot.astype(jnp.bfloat16),
        jnp.where(sooner, 1.0, 0.0).astype(jnp.bfloat16),
        preferred_element_type=jnp.float32,
    )
    slot = jnp.sum(hot * ahead, axis=0, keepdims=True)
    place_of = crop.astype(jnp.float32) * capacity + slot
    low_ahead = jnp.sum(jnp.where(expert < per_half, ahead, 0.0), axis=0, keepdims=True)
    low = crop < per_half
    low_count = jnp.sum(jnp.where(low, 1.0, 0.0), axis=1, keepdims=True)
    date = lax.broadcasted_iota(jnp.int32, (1, length), 1).astype(jnp.float32)
    rank = jnp.where(low, low_ahead, date - low_ahead)
    within = jnp.where(rank < half, half - 1 - rank, rank)
    crossed = jnp.where(within < half, within + half, within - half)
    row_for = (jnp.where(low, within, crossed), jnp.where(low, crossed, within))
    rows = lax.broadcasted_iota(jnp.int32, (length, length), 0).astype(jnp.float32)
    wide_place = jnp.broadcast_to(place_of, (EXPERTS, length)).astype(jnp.bfloat16)
    ordered = [
        lax.dot_general(
            wide_place,
            jnp.where(rows == row, 1.0, 0.0).astype(jnp.bfloat16),
            (((1,), (1,)), ((), ())),
            preferred_element_type=jnp.float32,
        )[:1]
        for row in row_for
    ]
    own_row = jnp.where(y == 0, row_for[0], row_for[1])
    count = jnp.broadcast_to(low_count, (1, length))
    lines = (ordered[0], ordered[1], own_row, count)
    place_in = jnp.where(rows == own_row, 1.0, 0.0).astype(jnp.bfloat16)
    return lines, place_in


def attend_heads(query, key_vecs, value_vecs, column, line, gain):
    length = query.shape[0]
    lanes = 2 * HEAD_DIM
    first = lax.broadcasted_iota(jnp.int32, (length, lanes), 1) < HEAD_DIM
    later = lax.broadcasted_iota(jnp.int32, (length, length), 0)
    causal = later >= lax.broadcasted_iota(jnp.int32, (length, length), 1)
    none = jnp.zeros((), jnp.bfloat16)
    outcome = []
    for pair in range(query.shape[1] // lanes):
        cut = slice(pair * lanes, (pair + 1) * lanes)
        chosen = query[:, cut]
        both_heads = jnp.concatenate(
            [jnp.where(first, chosen, none), jnp.where(first, none, chosen)], axis=0
        )
        scores = lax.dot_general(
            both_heads, key_vecs[:, cut], (((1,), (1,)), ((), ())), preferred_element_type=jnp.float32
        )
        weighted = []
        for side in range(2):
            head = 2 * pair + side
            gap = column[:, head : head + 1] - line[head : head + 1, :]
            fade = jnp.exp(jnp.where(causal, gap, -jnp.inf))
            weighted.append(
                (scores[side * length : (side + 1) * length] * fade).astype(jnp.bfloat16)
            )
        mixed = jnp.dot(
            jnp.concatenate(weighted, axis=0), value_vecs[:, cut], preferred_element_type=jnp.float32
        )
        both = jnp.where(first, mixed[:length], mixed[length:])
        square = both * both
        scale = [
            lax.rsqrt(jnp.sum(part, axis=-1, keepdims=True) / HEAD_DIM + 1e-05)
            for part in (jnp.where(first, square, 0.0), jnp.where(first, 0.0, square))
        ]
        outcome.append((both * jnp.where(first, scale[0], scale[1]) * gain[:, cut]).astype(jnp.bfloat16))
    return jnp.concatenate(outcome, axis=1)


def attend_here_kernel(
    x_any,
    crop_ref,
    decay_ref,
    attn_gain_ref,
    head_gain_ref,
    moe_gain_ref,
    query_any,
    key_any,
    value_any,
    w_out_any,
    resid_ref,
    routed_ref,
    info_ref,
    need_ref,
    tokens,
    normed,
    total_ref,
    padded,
    head_gain_rows,
    line_ref,
    column_ref,
    w_query,
    w_key,
    w_value,
    w_out,
    weight_sem,
    stay_sem,
    x_sem,
    info_sem,
    pass_sem,
):
    z, x, y, c = place()
    spot, column_of = z * NX + x, y * NC + c
    spots = NZ * NX
    steps, _, width = w_query.shape
    span = x_any.shape[1]
    length = tokens.shape[0]
    each = HEADS // steps

    barrier = pltpu.get_barrier_semaphore()
    others = [(lax.rem(spot + k, spots), column_of) for k in range(1, spots)]
    others += [partner(CORE, z, x, y, c), partner(BY_Y, z, x, y, c)]
    for other in others:
        pl.semaphore_signal(
            barrier, inc=1, device_id=other, device_id_type=pl.DeviceIdType.MESH
        )

    def load(k, j):
        src = (query_any, key_any, value_any, w_out_any)[k]
        dst = (w_query, w_key, w_value, w_out)[k]
        cut = pl.ds(j * width, width)
        return pltpu.make_async_copy(
            src.at[cut] if k == 3 else src.at[:, cut], dst.at[j], weight_sem.at[k, j]
        )

    for j in range(steps):
        for k in range(4):
            load(k, j).start()
    mine = pl.ds(pl.multiple_of(spot * span, span), span)
    stay = pltpu.make_async_copy(x_any.at[spot], tokens.at[mine], stay_sem)
    stay.start()
    per_half = EXPERTS // NY
    lines, place_in = position_rows(crop_ref[...], y, per_half, length // 4)
    for k, value in enumerate(lines):
        info_ref[y, c, spot, k : k + 1, :] = value.astype(jnp.int32)
    info_ref[y, c, spot, len(lines) :, :] = jnp.zeros((8 - len(lines), length), jnp.int32)
    pl.semaphore_wait(barrier, spots + 1)

    def remote(src, dst, send, arrive, target):
        return pltpu.make_async_remote_copy(
            src_ref=src,
            dst_ref=dst,
            send_sem=send,
            recv_sem=arrive,
            device_id=target,
            device_id_type=pl.DeviceIdType.MESH,
        )

    own_info = info_ref.at[y, c, spot]
    for k in range(1, spots):
        there = lax.rem(spot + k, spots)
        remote(own_info, own_info, info_sem.at[0], info_sem.at[1], (there, column_of)).start()
    for k in range(1, spots):
        there = lax.rem(spot + k, spots)
        remote(
            x_any.at[there], tokens.at[mine], x_sem.at[0], x_sem.at[1], (there, column_of)
        ).start()

    until = lax.broadcasted_iota(jnp.int32, (length, length), 0) <= lax.broadcasted_iota(
        jnp.int32, (length, length), 1
    )
    running = jnp.dot(
        decay_ref[...],
        jnp.where(until, 1.0, 0.0),
        preferred_element_type=jnp.float32,
        precision=lax.Precision.HIGHEST,
    )
    padded[...] = jnp.zeros_like(padded)
    padded[:HEADS] = running
    upright = jnp.transpose(padded[...])
    head_gain = head_gain_ref[...].reshape(1, D).astype(jnp.float32)
    for j in range(steps):
        head_gain_rows[j] = head_gain[:, j * width : (j + 1) * width]
        line_ref[j] = running[j * each : (j + 1) * each]
        column_ref[j] = upright[:, j * each : (j + 1) * each]

    def core_pass():
        return remote(
            info_ref.at[y, c], info_ref.at[y, c], pass_sem.at[0, 0], pass_sem.at[1, 0],
            partner(CORE, z, x, y, c),
        )

    def y_pass():
        return remote(
            info_ref.at[y], info_ref.at[y], pass_sem.at[0, 1], pass_sem.at[1, 1],
            partner(BY_Y, z, x, y, c),
        )

    came = info_ref.at[y, c, pl.ds(0, spots - 1)]
    remote(came, came, info_sem.at[0], info_sem.at[1], others[0]).wait_recv()
    core_pass().start()
    seven = tokens.at[pl.ds(0, (spots - 1) * span)]
    remote(seven, seven, x_sem.at[0], x_sem.at[1], others[0]).wait_recv()
    stay.wait()
    widened = tokens[...].astype(jnp.float32)
    scaled = widened * rms_scale(widened, 1e-05) * attn_gain_ref[...].reshape(1, D).astype(jnp.float32)
    normed[...] = scaled.astype(jnp.bfloat16)
    total_ref[...] = widened

    def one_step(j, carry):
        for k in range(4):
            load(k, j).wait()

        def project(ref):
            return jnp.dot(
                normed[...], ref[j], preferred_element_type=jnp.float32
            ).astype(jnp.bfloat16)

        heads = attend_heads(
            project(w_query),
            project(w_key),
            project(w_value),
            column_ref[j],
            line_ref[j],
            head_gain_rows[j],
        )
        total_ref[...] += jnp.dot(heads, w_out[j], preferred_element_type=jnp.float32)

        @pl.when(j == 0)
        def _():
            landed = info_ref.at[y, 1 - c]
            remote(landed, landed, pass_sem.at[0, 0], pass_sem.at[1, 0], others[-2]).wait_recv()
            y_pass().start()

        return carry

    lax.fori_loop(0, steps, one_step, 0)
    resid = total_ref[...].astype(jnp.bfloat16)
    resid_ref[...] = resid
    wide = resid.astype(jnp.float32)
    scaled = wide * rms_scale(wide, 1e-05) * moe_gain_ref[...].reshape(1, D).astype(jnp.float32)
    routed_ref[...] = jnp.dot(
        place_in, scaled.astype(jnp.bfloat16), preferred_element_type=jnp.float32
    ).astype(jnp.bfloat16)

    y_landed = info_ref.at[1 - y]
    remote(y_landed, y_landed, pass_sem.at[0, 1], pass_sem.at[1, 1], others[-1]).wait_recv()
    low_count = info_ref[:, :, :, 3:4, :].reshape(NY * NC * spots, length)
    need_ref[0, 0] = jnp.max(jnp.maximum(low_count, length - low_count))
    remote(seven, seven, x_sem.at[0], x_sem.at[1], others[0]).wait_send()
    sent = info_ref.at[y, c, pl.ds(0, spots - 1)]
    remote(sent, sent, info_sem.at[0], info_sem.at[1], others[0]).wait_send()
    core_pass().wait_send()
    y_pass().wait_send()


def attend_here(x_spans, crops, decay, attn_gain, head_gain, moe_gain, w_query, w_key, w_value, w_out):
    spots, span = x_spans.shape[0], x_spans.shape[1]
    length = spots * span
    steps = 6
    width = D // steps
    vmem = pl.BlockSpec(memory_space=pltpu.VMEM)
    any_space = pl.BlockSpec(memory_space=pl.ANY)
    dma = pltpu.SemaphoreType.DMA
    return pl.pallas_call(
        attend_here_kernel,
        out_shape=(
            jax.ShapeDtypeStruct((length, D), jnp.bfloat16),
            jax.ShapeDtypeStruct((length, D), jnp.bfloat16),
            jax.ShapeDtypeStruct((NY, NC, spots, 8, length), jnp.int32),
            jax.ShapeDtypeStruct((1, 1), jnp.int32),
        ),
        in_specs=[any_space] + [vmem] * 5 + [any_space] * 4,
        out_specs=(vmem, vmem, vmem, pl.BlockSpec(memory_space=pltpu.SMEM)),
        scratch_shapes=[
            pltpu.VMEM((length, D), jnp.bfloat16),
            pltpu.VMEM((length, D), jnp.bfloat16),
            pltpu.VMEM((length, D), jnp.float32),
            pltpu.VMEM((length, length), jnp.float32),
            pltpu.VMEM((steps, 1, width), jnp.float32),
            pltpu.VMEM((steps, HEADS // steps, length), jnp.float32),
            pltpu.VMEM((steps, length, HEADS // steps), jnp.float32),
            pltpu.VMEM((steps, D, width), jnp.bfloat16),
            pltpu.VMEM((steps, D, width), jnp.bfloat16),
            pltpu.VMEM((steps, D, width), jnp.bfloat16),
            pltpu.VMEM((steps, width, D), jnp.bfloat16),
            dma((4, steps)),
            dma,
            dma((2,)),
            dma((2,)),
            dma((2, 2)),
        ],
        compiler_params=pltpu.CompilerParams(
            collective_id=0, has_side_effects=True, vmem_limit_bytes=60 * 1024 * 1024
        ),
    )(x_spans, crops, decay, attn_gain, head_gain, moe_gain, w_query, w_key, w_value, w_out)


def order_of(i, z):
    nearer = z + 1 - 2 * (z % 2)
    far = jnp.where(z < 2, 2, 1)
    last = jnp.where(z < 2, 3, 0)
    return jnp.where(i == 0, z, jnp.where(i == 1, nearer, jnp.where(i == 2, far, last)))


def experts_kernel(
    kept,
    info_ref,
    routed_ref,
    resid_ref,
    w_gate_any,
    w_up_any,
    w_down_any,
    out_ref,
    tokens,
    w_gate,
    w_up,
    w_down,
    packed,
    terms,
    core_buf,
    e_buf,
    x_buf,
    up_buf,
    down_buf,
    full,
    weight_sem,
    send_sem,
    core_send,
    base_arrive,
    extra_arrive,
    core_arrive,
    term_sem,
    e_send,
    e_arrive,
    x_send,
    x_arrive,
    chain_sem,
    full_sem,
):
    z, x, y, c = place()
    length = routed_ref.shape[0]
    half = length // 2
    extra = kept - half
    experts, _, width = w_gate.shape
    capacity = length // 4
    held = experts * capacity
    first_slot = (y * NC + c) * held
    mine, beside = chip_of(z, x, y), chip_of(z, x, 1 - y)
    pieces = tuple(pl.ds(p * half // 2, half // 2) for p in range(2))
    base, more, whole = pl.ds(0, half), pl.ds(half, extra), pl.ds(0, kept)

    loads = [
        pltpu.make_async_copy(src, dst, weight_sem.at[k])
        for k, (src, dst) in enumerate(
            ((w_gate_any, w_gate), (w_up_any, w_up), (w_down_any, w_down))
        )
    ]
    for load in loads:
        load.start()
    tokens[c, mine] = routed_ref[...]
    greet(z, x, y, c)

    def remote(src, dst, send, arrive, kind):
        return pltpu.make_async_remote_copy(
            src_ref=src,
            dst_ref=dst,
            send_sem=send,
            recv_sem=arrive,
            device_id=partner(kind, z, x, y, c),
            device_id_type=pl.DeviceIdType.MESH,
        )

    def landed(block, arrive):
        remote(block, block, arrive, arrive, CORE).wait_recv()

    def left(block, sent):
        remote(block, block, sent, sent, CORE).wait_send()

    def base_to(kind, chip):
        block = tokens.at[c, chip, base]
        only_if(
            exists(kind, z),
            lambda: remote(block, block, send_sem.at[kind], base_arrive.at[chip], kind).start(),
        )

    def extra_to(chip):
        remote(
            tokens.at[c, chip, pl.ds(0, extra)],
            tokens.at[c, chip, more],
            send_sem.at[BY_Y],
            extra_arrive.at[chip],
            BY_Y,
        ).start()

    def to_core(bz, chip, part):
        block = tokens.at[c, chip, part]
        remote(block, block, core_send.at[bz], core_arrive.at[bz], CORE).start()

    def base_in(chip):
        landed(tokens.at[c, chip, base], base_arrive.at[chip])

    def spots(distance, body):
        if isinstance(distance, int) and distance == 0:
            body(z, None)
            return
        for sign, way in ((-1, Z_UP), (1, Z_DOWN)):
            bz = z + sign * distance
            inside = jnp.logical_and(bz >= 0, bz < NZ)
            pl.when(inside)(lambda bz=bz, way=way: body(bz, way))

    def along_z(distance, by):
        def body(bz, way):
            chip = chip_of(bz, x, by)
            base_in(chip)
            base_to(way, chip)
            base_to(BY_X, chip)
            extra_to(chip)
            to_core(bz, chip, base)

        spots(distance, body)

    def across_x(distance, by):
        def body(bz, _):
            chip = chip_of(bz, 1 - x, by)
            base_in(chip)
            extra_to(chip)
            to_core(bz, chip, base)

        spots(distance, body)

    def extras(distance):
        def body(bz, _):
            for bx, by in ((x, 1 - y), (x, y), (1 - x, y), (1 - x, 1 - y)):
                if isinstance(distance, int) and distance == 0 and bx is x and by is y:
                    continue
                chip = chip_of(bz, bx, by)
                landed(tokens.at[c, chip, more], extra_arrive.at[chip])
                to_core(bz, chip, more)

        spots(distance, body)

    def core_wait(bz):
        landed(tokens.at[1 - c, pl.ds(bz * LAYER, LAYER), whole], core_arrive.at[bz])

    slots = lax.broadcasted_iota(jnp.int32, (held, length), 0) + first_slot

    def select(bz, bx, by, core):
        hit = slots == info_ref[by, core, bz * NX + bx, pl.ds(y, 1), :]
        return jnp.where(hit, 1.0, 0.0).astype(jnp.bfloat16)[:, :kept]

    spread_over = [(bx, by) for bx in range(NX) for by in range(NY)]

    def pack(bz, core):
        for k, (bx, by) in enumerate(spread_over):
            picked = jnp.dot(
                select(bz, bx, by, core),
                tokens[core, chip_of(bz, bx, by), :kept],
                preferred_element_type=jnp.float32,
            ).astype(jnp.bfloat16)
            for j in range(experts):
                packed[j, core * LAYER + k] = picked[j * capacity : (j + 1) * capacity]

    def run_expert(j):
        given = packed[j].reshape(NC * LAYER * capacity, D)
        gate_act = jnp.dot(given, w_gate[j], preferred_element_type=jnp.float32)
        up_act = jnp.dot(given, w_up[j], preferred_element_type=jnp.float32)
        hidden = (gate_act / (1.0 + jnp.exp(-gate_act)) * up_act).astype(jnp.bfloat16)
        packed[j] = (
            jnp.dot(hidden, w_down[j], preferred_element_type=jnp.float32)
            .astype(jnp.bfloat16)
            .reshape(NC * LAYER, capacity, D)
        )

    def unpack(bz, core):
        for k, (bx, by) in enumerate(spread_over):
            term = jnp.concatenate(
                [packed[j, core * LAYER + k] for j in range(experts)], axis=0
            )
            terms[core, chip_of(bz, bx, by), :kept] = lax.dot_general(
                select(bz, bx, by, core),
                term,
                (((0,), (0,)), ((), ())),
                preferred_element_type=jnp.float32,
            ).astype(jnp.bfloat16)

    def term_copy(bz):
        layer = pl.ds(bz * LAYER, LAYER)
        return remote(
            terms.at[1 - c, layer, whole],
            core_buf.at[layer, whole],
            term_sem.at[0, bz],
            term_sem.at[1, bz],
            CORE,
        )

    def wide(ref, *index):
        return ref[index].astype(jnp.float32)

    def edges(bz):
        term_copy(bz).wait_recv()
        for bx, by in ((1 - x, 1 - y), (1 - x, y), (x, 1 - y), (x, y)):
            chip = chip_of(bz, bx, by)
            total = wide(core_buf, chip, more) + wide(terms, c, chip, more)
            core_buf[chip, more] = total.astype(jnp.bfloat16)
            remote(
                core_buf.at[chip, more], e_buf.at[chip], e_send, e_arrive.at[chip], BY_Y
            ).start()

    def planes(bz):
        for bx in (1 - x, x):
            for by in (1 - y, y):
                chip = chip_of(bz, bx, by)
                landed(e_buf.at[chip], e_arrive.at[chip])
                total = wide(core_buf, chip, base) + wide(terms, c, chip, base)
                near = total[:extra] + wide(e_buf, chip)
                core_buf[chip, pl.ds(0, extra)] = near.astype(jnp.bfloat16)
                if extra < half:
                    core_buf[chip, pl.ds(extra, half - extra)] = total[extra:].astype(jnp.bfloat16)
                if bx is not x:
                    for p, piece in enumerate(pieces):
                        remote(
                            core_buf.at[chip, piece],
                            x_buf.at[bz, by, piece],
                            x_send,
                            x_arrive.at[bz, by, p],
                            BY_X,
                        ).start()

    def chain_copy(by, bz, kind, p):
        block = (up_buf if kind == Z_UP else down_buf).at[by, bz, pieces[p]]
        return remote(
            block, block, chain_sem.at[0, kind, by, bz, p], chain_sem.at[1, kind, by, bz, p], kind
        )

    def in_plane(by, bz, p):
        landed(x_buf.at[bz, by, pieces[p]], x_arrive.at[bz, by, p])
        return wide(core_buf, chip_of(bz, x, by), pieces[p]) + wide(x_buf, bz, by, pieces[p])

    def along(bz):
        for by, p in ((1 - y, 0), (1 - y, 1), (y, 0), (y, 1)):
            total = in_plane(by, bz, p)
            for buf, kind, goes, comes in (
                (up_buf, Z_UP, bz > z, z > 0),
                (down_buf, Z_DOWN, bz < z, z < NZ - 1),
            ):

                @pl.when(goes)
                def _(by=by, p=p, total=total, buf=buf, kind=kind, comes=comes):
                    at = (by, bz, pieces[p])

                    @pl.when(comes)
                    def _():
                        chain_copy(by, bz, kind, p).wait_recv()
                        buf[at] = (total + wide(buf, *at)).astype(jnp.bfloat16)

                    @pl.when(jnp.logical_not(comes))
                    def _():
                        buf[at] = total.astype(jnp.bfloat16)

                    chain_copy(by, bz, kind, p).start()

    def finish(by, p, target):
        total = in_plane(by, z, p)
        at = (by, z, pieces[p])

        @pl.when(z == 0)
        def _():
            chain_copy(by, z, Z_DOWN, p).wait_recv()
            target[...] = (total + wide(down_buf, *at)).astype(jnp.bfloat16)

        @pl.when(z == NZ - 1)
        def _():
            chain_copy(by, z, Z_UP, p).wait_recv()
            target[...] = (total + wide(up_buf, *at)).astype(jnp.bfloat16)

        @pl.when(jnp.logical_and(z > 0, z < NZ - 1))
        def _():
            chain_copy(by, z, Z_DOWN, p).wait_recv()
            chain_copy(by, z, Z_UP, p).wait_recv()
            both = wide(up_buf, *at) + wide(down_buf, *at)
            target[...] = (total + both).astype(jnp.bfloat16)

    remote(
        tokens.at[c, mine, pl.ds(half, half)],
        tokens.at[c, mine, base],
        send_sem.at[CORE],
        base_arrive.at[mine],
        BY_Y,
    ).start()
    for kind in (Z_UP, Z_DOWN, BY_X):
        base_to(kind, mine)
    extra_to(mine)
    to_core(z, mine, whole)
    base_in(beside)
    for kind in (Z_UP, Z_DOWN, BY_X):
        base_to(kind, beside)
    to_core(z, beside, base)
    along_z(1, y)
    across_x(0, y)
    along_z(1, 1 - y)
    across_x(0, 1 - y)
    extras(0)
    core_wait(z)
    for load in loads:
        load.wait()

    def step(i, carry):
        bz = order_of(i, z)
        before = order_of(i - 1, z)
        @pl.when(i < 2)
        def _():
            along_z(i + 2, y)

        @pl.when(i < 3)
        def _():
            across_x(i + 1, y)

        @pl.when(i < 2)
        def _():
            along_z(i + 2, 1 - y)

        pack(bz, 0)

        pack(bz, 1)

        @pl.when(i == NZ - 1)
        def _():
            edges(before)

        run_expert(0)

        @pl.when(i < 3)
        def _():
            across_x(i + 1, 1 - y)

        run_expert(1)

        unpack(bz, 1 - c)

        term_copy(bz).start()

        @pl.when(i == NZ - 1)
        def _():
            planes(before)

        unpack(bz, c)

        @pl.when(i < 3)
        def _():
            extras(i + 1)
            core_wait(order_of(i + 1, z))

        return carry

    lax.fori_loop(0, NZ, step, 0)
    far, farthest, nearer = order_of(2, z), order_of(3, z), order_of(1, z)
    edge = jnp.logical_or(z == 0, z == NZ - 1)
    edges(farthest)
    edges(nearer)
    edges(z)
    pl.when(edge)(lambda: along(far))
    planes(farthest)
    pl.when(jnp.logical_not(edge))(lambda: along(far))
    planes(nearer)
    along(farthest)
    planes(z)
    along(nearer)
    gives = [
        remote(
            core_buf.at[beside, piece],
            full.at[pl.ds(half + p * half // 2, half // 2)],
            full_sem.at[0, p],
            full_sem.at[1, p],
            BY_Y,
        )
        for p, piece in enumerate(pieces)
    ]
    for p, piece in enumerate(pieces):
        finish(1 - y, p, core_buf.at[beside, piece])
        gives[p].start()
    for p, piece in enumerate(pieces):
        finish(y, p, full.at[piece])
    own_row = info_ref[y, c, z * NX + x, 2:3, :]
    rows = lax.broadcasted_iota(jnp.int32, (length, length), 0)
    place_in = jnp.where(rows == own_row, 1.0, 0.0).astype(jnp.bfloat16)
    for give in gives:
        give.wait_recv()
    expert_out = lax.dot_general(
        place_in, full[...], (((0,), (0,)), ((), ())), preferred_element_type=jnp.float32
    )
    out_ref[...] = (resid_ref[...].astype(jnp.float32) + expert_out).astype(jnp.bfloat16)

    left(tokens.at[0, 0, base], send_sem.at[CORE])
    left(e_buf.at[pl.ds(0, CHIPS - 1)], send_sem.at[BY_Y])
    left(tokens.at[0, pl.ds(0, NZ)], send_sem.at[BY_X])
    for count in range(1, NZ):
        pl.when(z == count - 1)(
            lambda count=count: left(tokens.at[0, pl.ds(0, count)], send_sem.at[Z_UP])
        )
        pl.when(z == NZ - count)(
            lambda count=count: left(tokens.at[0, pl.ds(0, count)], send_sem.at[Z_DOWN])
        )
    left(e_buf, e_send)
    left(x_buf, x_send)
    for give in gives:
        give.wait_send()
    for bz in range(NZ):
        layer = pl.ds(bz * LAYER, LAYER)
        left(tokens.at[0, layer, whole], core_send.at[bz])
        left(terms.at[0, layer, whole], term_sem.at[0, bz])
        for by in range(NY):
            for kind, goes in ((Z_UP, bz > z), (Z_DOWN, bz < z)):
                for p, piece in enumerate(pieces):
                    pl.when(goes)(
                        lambda by=by, bz=bz, kind=kind, p=p, piece=piece: left(
                            up_buf.at[by, bz, piece], chain_sem.at[0, kind, by, bz, p]
                        )
                    )


def routed_experts(kept, number, info, routed, resid, w_gate, w_up, w_down):
    length = routed.shape[0]
    capacity = length // 4
    half = length // 2
    local_count, _, width = w_gate.shape

    def vmem(*shape):
        return pltpu.VMEM(shape, jnp.bfloat16)

    dma = pltpu.SemaphoreType.DMA
    any_space = pl.BlockSpec(memory_space=pl.ANY)
    in_vmem = pl.BlockSpec(memory_space=pltpu.VMEM)
    return pl.pallas_call(
        functools.partial(experts_kernel, kept),
        out_shape=jax.ShapeDtypeStruct((length, D), jnp.bfloat16),
        in_specs=[in_vmem, in_vmem, in_vmem, any_space, any_space, any_space],
        out_specs=in_vmem,
        scratch_shapes=[
            vmem(NC, CHIPS, length, D),
            vmem(local_count, D, width),
            vmem(local_count, D, width),
            vmem(local_count, width, D),
            vmem(local_count, NC * LAYER, capacity, D),
            vmem(NC, CHIPS, length, D),
            vmem(CHIPS, length, D),
            vmem(CHIPS, kept - half, D),
            vmem(NZ, NY, half, D),
            vmem(NY, NZ, half, D),
            vmem(NY, NZ, half, D),
            vmem(length, D),
            dma((3,)),
            dma((5,)),
            dma((NZ,)),
            dma((CHIPS,)),
            dma((CHIPS,)),
            dma((NZ,)),
            dma((2, NZ)),
            dma,
            dma((CHIPS,)),
            dma,
            dma((NZ, NY, 2)),
            dma((2, 2, NY, NZ, 2)),
            dma((2, 2)),
        ],
        compiler_params=pltpu.CompilerParams(
            collective_id=number, has_side_effects=True, vmem_limit_bytes=60 * 1024 * 1024
        ),
    )(info, routed, resid, w_gate, w_up, w_down)


def here(x_spans, crops, decay, attn_gain, head_gain, moe_gain, w_query, w_key, w_value, w_out, w_gate, w_up, w_down):
    span = x_spans.shape[3]
    length = x_spans.shape[1] * span
    resid, routed, info, need = attend_here(
        x_spans.reshape(-1, span, D),
        crops.reshape(1, length),
        decay.reshape(length, HEADS).T,
        attn_gain,
        head_gain,
        moe_gain,
        w_query,
        w_key,
        w_value,
        w_out,
    )
    operands = (info, routed, resid, w_gate, w_up, w_down)
    shares = (length * 5 // 8, length * 3 // 4, length)
    way = sum((need[0, 0] > share).astype(jnp.int32) for share in shares[:-1])
    ways = [
        functools.partial(routed_experts, share, number)
        for number, share in enumerate(shares, start=1)
    ]
    return lax.switch(way, ways, *operands).reshape(1, 1, length, D)


def on_device(
    x_spans,
    crops,
    decay,
    attn_gain,
    w_query,
    w_key,
    w_value,
    head_gain,
    w_out,
    moe_gain,
    w_gate,
    w_up,
    w_down,
):
    if lax.axis_size("dp") == NZ * NX and lax.axis_size("expert") == NY * NC:
        return here(
            x_spans,
            crops,
            decay,
            attn_gain,
            head_gain,
            moe_gain,
            w_query,
            w_key,
            w_value,
            w_out,
            w_gate,
            w_up,
            w_down,
        )
    arrived = lax.all_to_all(x_spans, "dp", split_axis=1, concat_axis=0, tiled=True)
    length = arrived.shape[0] * arrived.shape[3]
    tokens = arrived.reshape(length, D)
    forget = decay.reshape(length, HEADS)
    crop_ids = crops.reshape(length)
    capacity = length // 4
    position = slot_positions(crop_ids, capacity)
    resid, routed = attend(
        tokens, forget, attn_gain, w_query, w_key, w_value, head_gain, w_out, moe_gain
    )
    resid_wide = resid.astype(jnp.float32)
    select = (jnp.arange(EXPERTS * capacity, dtype=jnp.int32)[:, None] == position[None, :]).astype(
        jnp.bfloat16
    )
    packed = jnp.dot(select, routed, preferred_element_type=jnp.float32).astype(jnp.bfloat16)
    owners = lax.axis_size("expert")
    local_count = w_gate.shape[0]
    outgoing = packed.reshape(1, owners, EXPERTS * capacity // owners, D)
    gathered = spread(deliver(outgoing))
    sources = gathered.shape[0]
    grouped = gathered.reshape(sources, owners, local_count, capacity, D)
    gate_act = jnp.einsum("sojcd,jdf->sojcf", grouped, w_gate, preferred_element_type=jnp.float32)
    up_act = jnp.einsum("sojcd,jdf->sojcf", grouped, w_up, preferred_element_type=jnp.float32)
    hidden = (jax.nn.silu(gate_act) * up_act).astype(jnp.bfloat16)
    term = jnp.einsum("sojcf,jfd->sojcd", hidden, w_down, preferred_element_type=jnp.float32)
    summed = lax.psum_scatter(
        term.reshape(1 * lax.axis_size("dp"), owners, local_count * capacity, D).astype(
            jnp.bfloat16
        ),
        "dp",
        scatter_dimension=0,
        tiled=True,
    )
    own_sums = summed[0]
    returned = lax.all_to_all(own_sums, "expert", split_axis=0, concat_axis=0, tiled=True)
    flat_back = returned.reshape(EXPERTS * capacity, D)
    expert_out = jnp.einsum("pl,pd->ld", select, flat_back, preferred_element_type=jnp.float32)
    layer_sum = (resid_wide + expert_out).astype(jnp.bfloat16)
    return layer_sum.reshape(1, 1, length, D)


def solution(mesh):
    return jax.shard_map(
        on_device,
        mesh=mesh,
        in_specs=(
            P("dp", None, "expert", None, None),
            P("dp", "expert", None, None),
            P("dp", "expert", None, None),
            P(),
            P(),
            P(),
            P(),
            P(),
            P(),
            P(),
            P("expert", None, "dp"),
            P("expert", None, "dp"),
            P("expert", "dp", None),
        ),
        out_specs=P("dp", "expert", None, None),
        check_vma=False,
    )
```
